512 devices in a mesh: req: 16 (over y_hi, z), cand: 32 (over x, y_lo, core).
Axes of the slice: x: 4, y: 8 (y_hi: 2, y_lo: 4; y = y_hi * 4 + y_lo), z: 8, core: 2. Of those that a mesh axis runs over, the one named last changes fastest.
Arguments:
- dense_feat: bfloat16 [65536, 512], P(('req', 'cand')), may hold values from -6 to 6
- emb_ids: int32 [32, 4, 65536], P('cand', None, 'req'), may hold values from 0 to 32767
- tables: bfloat16 [32, 16, 32768], P('cand'), may hold values from -3 to 3
- history_kv: bfloat16 [32, 64, 2048], P('req', 'cand'), may hold values from -6 to 6
- hist_len: int32 [32], P('req'), may hold values from 1 to 64, 1024 in all
- cand_request: int32 [65536], P(('req', 'cand')), may hold values from 0 to 1
- w_query: bfloat16 [1024, 1024], P(('req', 'cand')), may hold values from -0.1875 to 0.1875
- w_out: bfloat16 [1024, 1024], P(('req', 'cand')), may hold values from -0.1875 to 0.1875
- cotangent: bfloat16 [65536, 1024], P(('req', 'cand')), may hold values from -2 to 2
Outputs:
- cand_out: bfloat16 [65536, 1024], P(('req', 'cand'))
- d_kv: float32 [32, 64, 2048], P('req', 'cand')
- d_pooled: bfloat16 [32, 16, 65536], P('cand', None, 'req')
The draws below stay inside these ranges and needn't reach their ends.
Inputs may be any that keep to these rules, and one draw needn't show every extreme that they name: `hist_len`: the lengths sum to 1024 and the largest equals 64.
All inputs are finite; a program needn't handle non-finite values. No bound on the sum of `hist_len` on one device may be relied on, other than what follows from the above.
Results may differ from the reference program's by a relative error of at most 0.023.
Values may be sent and summed in bfloat16 or wider, within the bound.
No kernel may reach another device: no remote copies, remote signals or barrier semaphores. Data moves between devices by JAX's collectives and lax.ppermute only.
A program may use at most 64 MiB of HBM per device.

```python
import math
import jax
import jax.numpy as jnp
import numpy as np
from jax import lax

D = 1024
H = 8
EMB = 16
TABLES = 32
DENSE = 512
ROWS = 32768
BAG = 4
REQ_OWN = 2
HIST = 64
CAND_DEV = 128
NREQ = 32
CANDS = 65536
N_REQ = 16
N_CAND = 32


def set_ends(result, rng, low, largest):
    spot = [jax.random.randint(jax.random.fold_in(rng, axis), (), 0, length) for axis, length in enumerate(result.shape)]
    main_axis = result.shape.index(max(result.shape))
    next_to = spot[:main_axis] + [(spot[main_axis] + 1) % result.shape[main_axis]] + spot[main_axis + 1:]
    return result.at[tuple(spot)].set(low).at[tuple(next_to)].set(largest)


def levels(rng, shape, cuts, smallest, high):
    loudness = 1.0
    for dim, blocks in cuts:
        steps = jax.random.uniform(jax.random.fold_in(jax.random.fold_in(rng, 6), dim), (blocks,), jnp.float32, smallest / len(cuts), high / len(cuts))
        loudness = loudness * jnp.repeat(jnp.exp(steps), shape[dim] // blocks).reshape((-1,) + (1,) * (len(shape) - 1 - dim))
    return loudness


def rank_bounds(count, lean):
    portions = [(1 << 20) // math.isqrt(grade ** lean) + 1 for grade in range(1, count + 1)]
    scale = 1 + sum(portions) // (1 << 30)
    return np.cumsum(np.array([max(1, weight // scale) for weight in portions]))


def skewed_ids(own_key, extent, number_of, slope):
    grid = rank_bounds(number_of, slope)
    pick = jax.random.randint(jax.random.fold_in(own_key, 1), extent, 0, int(grid[number_of - 1]))
    rank = jnp.searchsorted(jnp.asarray(grid, jnp.int32), pick, side="right")
    return jax.random.permutation(jax.random.fold_in(own_key, 2), number_of)[rank].astype(jnp.int32)


def profile(count, total, reach, skew):
    loads = [(1 << 20) // math.isqrt(rank ** skew) + 1 for rank in range(2, count + 1)]
    rest, counts = total - reach - (count - 1), [1] * (count - 1)
    while rest > 0:
        movable = [i for i in range(count - 1) if counts[i] < reach]
        whole, remaining = sum([loads[i] for i in movable]), rest
        for i in movable:
            more = min(reach - counts[i], max(1, remaining * loads[i] // whole), rest)
            counts[i] = counts[i] + more
            rest = rest - more
    return np.array([reach] + counts)


def ragged(key, count, total, reach, lean):
    if count == 2:
        one = jax.random.randint(key, (), max(1, total - reach), min(reach, total - 1) + 1)
        return jnp.stack([one, total - one])
    sizes = jnp.asarray(profile(count, total, reach, lean), jnp.int32)
    pairs = (count - 1) // 2
    donor, sink = sizes[1:1 + 2 * pairs:2], sizes[2:2 + 2 * pairs:2]
    slack = jnp.minimum(donor - 1, reach - sink)
    shifted = jax.random.randint(jax.random.fold_in(key, 1), (pairs,), 0, 1 << 20) % (slack + 1)
    sizes = sizes.at[1:1 + 2 * pairs:2].set(donor - shifted).at[2:2 + 2 * pairs:2].set(sink + shifted)
    return sizes[jax.random.permutation(jax.random.fold_in(key, 2), count)]


def gaussian(key, shape, spread, most, cuts=(), kind=jnp.bfloat16):
    factor_of = levels(key, shape, cuts, -0.22, 0.18) if cuts else 1.0
    drawn = jax.random.normal(key, shape, jnp.float32) * spread * factor_of
    return jnp.minimum(jnp.maximum(drawn, -most), most).astype(kind)


def setup_inputs(seed: int = 0) -> dict:
    keys = jax.random.split(jax.random.key(seed), 10)
    return {
        "dense_feat": gaussian(keys[0], (CANDS, DENSE), 1.0, 6.0, ((0, 512),)),
        "emb_ids": set_ends(skewed_ids(keys[1], (TABLES, BAG, CANDS), ROWS, 2), jax.random.fold_in(keys[1], 3), 0, ROWS - 1).astype(jnp.int32),
        "tables": gaussian(keys[2], (TABLES, EMB, ROWS), 0.5, 3.0, ((0, 32),)),
        "history_kv": gaussian(keys[3], (NREQ, HIST, 2 * D), 1.0, 6.0, ((0, 16), (1, 32))),
        "hist_len": ragged(keys[4], NREQ, NREQ * HIST // 2, HIST, 2).astype(jnp.int32),
        "cand_request": set_ends(jax.random.randint(keys[5], (CANDS,), 0, REQ_OWN), jax.random.fold_in(keys[5], 1), 0, REQ_OWN - 1).astype(jnp.int32),
        "w_query": gaussian(keys[6], (D, D), D ** -0.5, 0.1875, ((0, 512),)),
        "w_out": gaussian(keys[7], (D, D), D ** -0.5, 0.1875, ((0, 512),)),
        "cotangent": gaussian(keys[8], (CANDS, D), 0.25, 2.0, ((0, 512),)),
    }


norm_eps = 1e-05

def silu_slope(argument):
    sigmoid_value = jax.nn.sigmoid(argument)
    return sigmoid_value * (1.0 + argument * (1.0 - sigmoid_value))

def rounded(argument):
    return lax.optimization_barrier(argument.astype(jnp.bfloat16)).astype(jnp.float32)

def take_columns(table, indices):
    return jnp.take(table, indices, axis=1)

def device_step(features, requests, history, lengths, back_cot, w_query, w_out):
    cand_count, model_width = features.shape
    owned_count, hist_events, kv_width = history.shape
    events = owned_count * hist_events
    head_dim = model_width // H
    score_scale = 1.0 / math.sqrt(head_dim)
    pooled_width = TABLES * EMB
    query_pre = jnp.dot(features, w_query, preferred_element_type=jnp.float32)
    query_heads = rounded(jax.nn.silu(query_pre)).reshape(cand_count, H, head_dim)
    flat_events = history.reshape(events, kv_width).astype(jnp.float32)
    key_heads = flat_events[:, :model_width].reshape(events, H, head_dim)
    value_heads = flat_events[:, model_width:].reshape(events, H, head_dim)
    owner = (jnp.arange(events) // hist_events).astype(jnp.int32)
    position = (jnp.arange(events) % hist_events).astype(jnp.int32)
    in_length = position < lengths[owner]
    live_mask = ((requests[:, None] == owner[None, :]) & in_length[None, :]).astype(jnp.float32)
    scores = jnp.einsum('chd,ehd->che', query_heads, key_heads) * score_scale
    weights = rounded(jax.nn.silu(scores) * live_mask[:, None, :])
    attended = jnp.einsum('che,ehd->chd', weights, value_heads).reshape(cand_count, model_width)
    centered = attended - lax.optimization_barrier(jnp.mean(attended, axis=1, keepdims=True))
    inverse = lax.rsqrt(lax.optimization_barrier(jnp.mean(centered * centered, axis=1, keepdims=True)) + norm_eps)
    normed = centered * inverse
    mixed_out = jnp.dot(normed.astype(jnp.bfloat16), w_out, preferred_element_type=jnp.float32)
    cand_out = (mixed_out + features.astype(jnp.float32)).astype(jnp.bfloat16)
    back_y = jnp.dot(back_cot, w_out.T, preferred_element_type=jnp.float32)
    back_att = inverse * (back_y - lax.optimization_barrier(jnp.mean(back_y, axis=1, keepdims=True)) - normed * lax.optimization_barrier(jnp.mean(back_y * normed, axis=1, keepdims=True)))
    back_att = rounded(back_att).reshape(cand_count, H, head_dim)
    back_w = jnp.einsum('chd,ehd->che', back_att, value_heads)
    back_s = rounded(back_w * live_mask[:, None, :] * silu_slope(scores) * score_scale)
    back_query = jnp.einsum('che,ehd->chd', back_s, key_heads).reshape(cand_count, model_width)
    key_part = jnp.einsum('che,chd->ehd', back_s, query_heads).reshape(events, model_width)
    value_part = jnp.einsum('che,chd->ehd', weights, back_att).reshape(events, model_width)
    kv_part = jnp.concatenate([key_part, value_part], axis=1).astype(jnp.bfloat16)
    back_pre = (back_query * silu_slope(query_pre)).astype(jnp.bfloat16)
    back_pool = back_cot[:, :pooled_width].astype(jnp.float32) + jnp.dot(back_pre, w_query[:pooled_width].T, preferred_element_type=jnp.float32)
    return (cand_out, kv_part.reshape(owned_count, hist_events, kv_width), back_pool.astype(jnp.bfloat16))

def reference(dense_feat, emb_ids, tables, history_kv, hist_len, cand_request, w_query, w_out, cotangent):
    group_size = CAND_DEV * N_CAND

    def one_row(row_index):
        first_cand = (row_index * group_size).astype(jnp.int32)
        first_req = (row_index * REQ_OWN).astype(jnp.int32)
        row_ids = lax.dynamic_slice_in_dim(emb_ids, first_cand, group_size, 2)
        looked_up = jax.vmap(take_columns)(tables, row_ids)
        pooled = lax.optimization_barrier(jnp.sum(looked_up.astype(jnp.float32), axis=2)).astype(jnp.bfloat16)
        pooled = jnp.transpose(pooled, (2, 0, 1)).reshape(group_size, TABLES * EMB)
        features = jnp.concatenate([pooled, lax.dynamic_slice_in_dim(dense_feat, first_cand, group_size, 0)], axis=1)
        history = lax.dynamic_slice_in_dim(history_kv, first_req, REQ_OWN, 0)
        lengths = lax.dynamic_slice_in_dim(hist_len, first_req, REQ_OWN, 0)
        requests = lax.dynamic_slice_in_dim(cand_request, first_cand, group_size, 0)
        back_cot = lax.dynamic_slice_in_dim(cotangent, first_cand, group_size, 0)

        def one_device(device_index):
            first_row = (device_index * CAND_DEV).astype(jnp.int32)
            return device_step(lax.dynamic_slice_in_dim(features, first_row, CAND_DEV, 0), lax.dynamic_slice_in_dim(requests, first_row, CAND_DEV, 0), history, lengths, lax.dynamic_slice_in_dim(back_cot, first_row, CAND_DEV, 0), w_query, w_out)
        row_outputs, kv_parts, pool_grads = lax.map(one_device, jnp.arange(N_CAND, dtype=jnp.int32))
        kv_total = lax.optimization_barrier(jnp.sum(kv_parts.astype(jnp.float32), axis=0))
        return (row_outputs.reshape(group_size, D), kv_total, pool_grads.reshape(group_size, TABLES * EMB))
    row_outputs, kv_grads, pool_grads = lax.map(one_row, jnp.arange(N_REQ, dtype=jnp.int32))
    d_pooled = jnp.transpose(pool_grads.reshape(CANDS, TABLES * EMB), (1, 0)).reshape(TABLES, EMB, CANDS)
    return (row_outputs.reshape(CANDS, D), kv_grads.reshape(NREQ, HIST, 2 * D), d_pooled)
```

```python
import math

import jax
import jax.numpy as jnp
from jax import lax
from jax.experimental import pallas as pl
from jax.experimental.pallas import tpu as pltpu
from jax.sharding import Mesh, PartitionSpec as P


H = 8
norm_eps = 1e-05

REQ = ("yh", "z")
CAND = ("x", "yl", "core")
ALL = REQ + CAND

LOW = 512
TILE = 256


def pooled_lookup(ids, table):
    bag, count = ids.shape
    emb, rows = table.shape
    highs = rows // LOW
    step = min(count, 4 * TILE)

    def kernel(ids_ref, table_ref, out_ref, stacked_ref):
        @pl.when(pl.program_id(0) == 0)
        def _():
            for high in range(highs):
                stacked_ref[high * emb : (high + 1) * emb, :] = table_ref[:, high * LOW : (high + 1) * LOW]

        low_iota = lax.broadcasted_iota(jnp.int32, (LOW, TILE), 0)
        for tile in range(step // TILE):
            span = slice(tile * TILE, (tile + 1) * TILE)
            total = jnp.zeros((emb, TILE), jnp.float32)
            for slot in range(bag):
                row = ids_ref[slot : slot + 1, span]
                low = jnp.bitwise_and(row, LOW - 1)
                high_of = jnp.broadcast_to(jnp.right_shift(row, LOW.bit_length() - 1), (emb, TILE))
                one_hot = (low_iota == low).astype(jnp.float32).astype(jnp.bfloat16)
                picked = jnp.dot(stacked_ref[...], one_hot, preferred_element_type=jnp.float32)
                found = jnp.zeros((emb, TILE), jnp.float32)
                for high in range(highs):
                    found = jnp.where(high_of == high, picked[high * emb : (high + 1) * emb, :], found)
                total = total + found
            out_ref[:, span] = total.astype(jnp.bfloat16)

    return pl.pallas_call(
        kernel,
        grid=(count // step,),
        in_specs=[
            pl.BlockSpec((bag, step), lambda i: (0, i)),
            pl.BlockSpec((emb, rows), lambda i: (0, 0)),
        ],
        out_specs=pl.BlockSpec((emb, step), lambda i: (0, i)),
        out_shape=jax.ShapeDtypeStruct((emb, count), jnp.bfloat16),
        scratch_shapes=[pltpu.VMEM((highs * emb, LOW), jnp.bfloat16)],
        compiler_params=pltpu.CompilerParams(vmem_limit_bytes=32 << 20),
        cost_estimate=pl.CostEstimate(
            flops=2 * emb * rows * bag * count, bytes_accessed=2 * emb * rows, transcendentals=0
        ),
        name="pooled_lookup",
    )(ids, table)


def dot_nn(left, right):
    return jnp.dot(left, right, preferred_element_type=jnp.float32)


def dot_nt(left, right):
    return lax.dot_general(left, right, (((1,), (1,)), ((), ())), preferred_element_type=jnp.float32)


def dot_tn(left, right):
    return lax.dot_general(left, right, (((0,), (0,)), ((), ())), preferred_element_type=jnp.float32)


def layer(pooled_t, dense, cot, mine, other, core, events, requests, lengths):
    pooled_width, cands = pooled_t.shape
    outer, middle, inner, width = mine.shape
    dim = width // H
    event_count = events.shape[0]
    owned = lengths.shape[0]
    scale = 1.0 / math.sqrt(dim)

    def kernel(
        core_ref, len_ref, pt_ref, dense_ref, cot_ref, mine_ref, other_ref, ev_ref, req_ref,
        out_ref, kv_ref, pool_ref, wq_ref, wo_ref,
    ):
        def place(source, target):
            for i in range(middle):
                for j in range(outer):
                    start = (i * outer + j) * inner
                    target[start : start + inner, :] = source[j, i]

        @pl.when(core_ref[0] == 0)
        def _():
            place(mine_ref, wq_ref)
            place(other_ref, wo_ref)

        @pl.when(core_ref[0] != 0)
        def _():
            place(other_ref, wq_ref)
            place(mine_ref, wo_ref)

        pooled = jnp.transpose(pt_ref[...].astype(jnp.float32))
        query_pre = dot_nn(pooled.astype(jnp.bfloat16), wq_ref[:pooled_width, :]) + dot_nn(
            dense_ref[...], wq_ref[pooled_width:, :]
        )
        gate = jax.nn.sigmoid(query_pre)
        query = (query_pre * gate).astype(jnp.bfloat16)
        query_slope = gate * (1.0 + query_pre * (1.0 - gate))

        index = lax.broadcasted_iota(jnp.int32, (cands, event_count), 1)
        owner = index % owned
        limit = jnp.full((cands, event_count), len_ref[0], jnp.int32)
        for a in range(1, owned):
            limit = jnp.where(owner == a, len_ref[a], limit)
        live = ((owner == req_ref[...]) & (index // owned < limit)).astype(jnp.float32)

        weights, slopes, attended = [], [], []
        for h in range(H):
            cols = slice(h * dim, (h + 1) * dim)
            vcols = slice(width + h * dim, width + (h + 1) * dim)
            score = dot_nt(query[:, cols], ev_ref[:, cols]) * scale
            sig = jax.nn.sigmoid(score)
            weight = (score * sig * live).astype(jnp.bfloat16)
            weights.append(weight)
            slopes.append(live * (sig * (1.0 + score * (1.0 - sig))) * scale)
            attended.append(dot_nn(weight, ev_ref[:, vcols]))
        attended = jnp.concatenate(attended, axis=1)
        centered = attended - jnp.mean(attended, axis=1, keepdims=True)
        inverse = lax.rsqrt(jnp.mean(centered * centered, axis=1, keepdims=True) + norm_eps)
        normed = centered * inverse
        mixed = dot_nn(normed.astype(jnp.bfloat16), wo_ref[...])
        out_ref[:, :pooled_width] = (mixed[:, :pooled_width] + pooled).astype(jnp.bfloat16)
        out_ref[:, pooled_width:] = (mixed[:, pooled_width:] + dense_ref[...].astype(jnp.float32)).astype(
            jnp.bfloat16
        )
        back_y = dot_nt(cot_ref[...], wo_ref[...])
        back_att = inverse * (
            back_y
            - jnp.mean(back_y, axis=1, keepdims=True)
            - normed * jnp.mean(back_y * normed, axis=1, keepdims=True)
        )
        back_att = back_att.astype(jnp.bfloat16)
        back_query = []
        for h in range(H):
            cols = slice(h * dim, (h + 1) * dim)
            vcols = slice(width + h * dim, width + (h + 1) * dim)
            back_w = dot_nt(back_att[:, cols], ev_ref[:, vcols])
            back_s = (back_w * slopes[h]).astype(jnp.bfloat16)
            back_query.append(dot_nn(back_s, ev_ref[:, cols]))
            kv_ref[:, cols] = dot_tn(back_s, query[:, cols]).astype(jnp.bfloat16)
            kv_ref[:, vcols] = dot_tn(weights[h], back_att[:, cols]).astype(jnp.bfloat16)
        back_pre = (jnp.concatenate(back_query, axis=1) * query_slope).astype(jnp.bfloat16)
        columns = dot_nt(wq_ref[:pooled_width, :], back_pre)
        pool_ref[...] = (jnp.transpose(cot_ref[:, :pooled_width].astype(jnp.float32)) + columns).astype(
            jnp.bfloat16
        )

    vmem = pl.BlockSpec(memory_space=pltpu.VMEM)
    return pl.pallas_call(
        kernel,
        in_specs=[pl.BlockSpec(memory_space=pltpu.SMEM)] * 2 + [vmem] * 7,
        out_specs=[vmem] * 3,
        out_shape=[
            jax.ShapeDtypeStruct((cands, width), jnp.bfloat16),
            jax.ShapeDtypeStruct((event_count, 2 * width), jnp.bfloat16),
            jax.ShapeDtypeStruct((pooled_width, cands), jnp.bfloat16),
        ],
        scratch_shapes=[pltpu.VMEM((width, width), jnp.bfloat16)] * 2,
        compiler_params=pltpu.CompilerParams(vmem_limit_bytes=40 << 20),
        cost_estimate=pl.CostEstimate(
            flops=8 * cands * width * width, bytes_accessed=8 * width * width, transcendentals=0
        ),
        name="layer",
    )(core, lengths, pooled_t, dense, cot, mine, other, events, requests)


def spread(block, axes):
    size = math.prod(lax.axis_size(a) for a in axes)
    return lax.all_to_all(jnp.broadcast_to(block[None], (size,) + block.shape), axes, 0, 0)


def on_device(dense_feat, emb_ids, tables, history_kv, hist_len, cand_request, w_query, w_out, cotangent):
    _, emb_width, _ = tables.shape
    sizes = {a: lax.axis_size(a) for a in ALL}
    cand_devices = sizes["x"] * sizes["yl"] * sizes["core"]
    own_rows, model_width = w_query.shape
    owned, own_events, kv_width = history_kv.shape
    group = emb_ids.shape[2]
    cands = group // cand_devices

    own = jnp.concatenate([w_query, w_out], axis=0).reshape(1, 2, own_rows, model_width)
    slab = sizes["yh"] * sizes["z"] * sizes["yl"]
    own = jnp.broadcast_to(own, (slab, 2, own_rows, model_width)).reshape(2 * slab, own_rows, model_width)
    w1 = lax.all_to_all(own, ("yh", "z", "yl", "core"), 0, 0).reshape(2 * slab * own_rows, model_width)
    own_hist = jnp.transpose(history_kv, (1, 0, 2)).reshape(own_events * owned, kv_width)
    events = spread(own_hist, CAND).reshape(cand_devices * own_events * owned, kv_width)

    pooled_rows = pooled_lookup(emb_ids[0], tables[0])

    mine = spread(w1, ("x",))
    mine = mine.reshape(sizes["x"], sizes["yh"] * sizes["z"], -1, model_width)
    other = lax.ppermute(mine, "core", [(0, 1), (1, 0)])

    sent = jnp.transpose(pooled_rows.reshape(emb_width, cand_devices, cands), (1, 0, 2))
    pooled_t = lax.all_to_all(sent, CAND, 0, 0).reshape(-1, cands)

    cand_out, kv_part, back_pool = layer(
        pooled_t,
        dense_feat,
        cotangent,
        mine,
        other,
        lax.axis_index("core").reshape(1),
        events,
        cand_request.reshape(-1, 1),
        hist_len,
    )

    own = own_events * owned
    joined = jnp.concatenate(
        [kv_part.reshape(cand_devices, own, kv_width), back_pool.reshape(cand_devices, own, -1)], axis=2
    )
    back = lax.all_to_all(joined, CAND, 0, 0)
    d_kv = jnp.sum(back[:, :, :kv_width].astype(jnp.float32), axis=0)
    d_kv = jnp.transpose(d_kv.reshape(own_events, owned, kv_width), (1, 0, 2))
    pool_all = back[:, :, kv_width:].reshape(cand_devices, emb_width, cands)
    d_pooled = jnp.transpose(pool_all, (1, 0, 2)).reshape(1, emb_width, group)
    return cand_out, d_kv, d_pooled


def solution(mesh):
    parts = Mesh(mesh.devices.reshape(2, 8, 4, 4, 2), ALL)
    rows = P(ALL, None)
    return jax.shard_map(
        on_device,
        mesh=parts,
        in_specs=(
            rows,
            P(CAND, None, REQ),
            P(CAND, None, None),
            P(REQ, CAND, None),
            P(REQ),
            P(ALL),
            rows,
            rows,
            rows,
        ),
        out_specs=(rows, P(REQ, CAND, None), P(CAND, None, REQ)),
        check_vma=False,
    )
```

```python
import math

import jax
import jax.numpy as jnp
from jax import lax
from jax.experimental import pallas as pl
from jax.experimental.pallas import tpu as pltpu
from jax.sharding import Mesh, PartitionSpec as P


H = 8
norm_eps = 1e-05

REQ = ("yh", "z")
CAND = ("x", "yl", "core")
ALL = REQ + CAND


LOW = 512
TILE = 256


def pooled_lookup(ids, table):
    bag, count = ids.shape
    emb, rows = table.shape
    highs = rows // LOW
    step = min(count, 4 * TILE)

    def kernel(ids_ref, table_ref, out_ref, stacked_ref):
        @pl.when(pl.program_id(0) == 0)
        def _():
            for high in range(highs):
                stacked_ref[high * emb : (high + 1) * emb, :] = table_ref[:, high * LOW : (high + 1) * LOW]

        low_iota = lax.broadcasted_iota(jnp.int32, (LOW, TILE), 0)
        for tile in range(step // TILE):
            span = slice(tile * TILE, (tile + 1) * TILE)
            total = jnp.zeros((emb, TILE), jnp.float32)
            for slot in range(bag):
                row = ids_ref[slot : slot + 1, span]
                low = jnp.bitwise_and(row, LOW - 1)
                high_of = jnp.broadcast_to(jnp.right_shift(row, LOW.bit_length() - 1), (emb, TILE))
                one_hot = (low_iota == low).astype(jnp.float32).astype(jnp.bfloat16)
                picked = jnp.dot(stacked_ref[...], one_hot, preferred_element_type=jnp.float32)
                found = jnp.zeros((emb, TILE), jnp.float32)
                for high in range(highs):
                    found = jnp.where(high_of == high, picked[high * emb : (high + 1) * emb, :], found)
                total = total + found
            out_ref[:, span] = total.astype(jnp.bfloat16)

    return pl.pallas_call(
        kernel,
        grid=(count // step,),
        in_specs=[
            pl.BlockSpec((bag, step), lambda i: (0, i)),
            pl.BlockSpec((emb, rows), lambda i: (0, 0)),
        ],
        out_specs=pl.BlockSpec((emb, step), lambda i: (0, i)),
        out_shape=jax.ShapeDtypeStruct((emb, count), jnp.bfloat16),
        scratch_shapes=[pltpu.VMEM((highs * emb, LOW), jnp.bfloat16)],
        compiler_params=pltpu.CompilerParams(vmem_limit_bytes=32 << 20),
        cost_estimate=pl.CostEstimate(
            flops=2 * emb * rows * bag * count, bytes_accessed=2 * emb * rows, transcendentals=0
        ),
        name="pooled_lookup",
    )(ids, table)


def dot_nn(left, right):
    return jnp.dot(left, right, preferred_element_type=jnp.float32)


def dot_nt(left, right):
    return lax.dot_general(left, right, (((1,), (1,)), ((), ())), preferred_element_type=jnp.float32)


def dot_tn(left, right):
    return lax.dot_general(left, right, (((0,), (0,)), ((), ())), preferred_element_type=jnp.float32)


def layer(pooled_t, dense, cot, mine, other, place_index, events, requests, lengths):
    pooled_width, cands = pooled_t.shape
    own_shape, _, _ = (piece.shape for piece in mine)
    width = own_shape[1]
    block = own_shape[0]
    outer = width // block
    inner = 16
    dim = width // H
    event_count = events.shape[0]
    owned = lengths.shape[0]
    scale = 1.0 / math.sqrt(dim)

    def kernel(
        place_ref, len_ref, pt_ref, dense_ref, cot_ref,
        own_a, sides_a, far_a, own_b, sides_b, far_b, ev_ref, req_ref,
        out_ref, kv_ref, pool_ref, wq_ref, wo_ref,
    ):
        x = place_ref[1]

        def place(own, sides, far, target):
            def put(source, first, offset):
                for i in range(source.shape[0] // inner):
                    start = pl.multiple_of(((first + i) * outer + lax.rem(x + offset, outer)) * inner, inner)
                    target[pl.ds(start, inner), :] = source[i * inner : (i + 1) * inner, :]

            put(own, 0, 0)
            put(sides.at[0], 0, outer - 1)
            put(sides.at[1], 0, 1)
            half = block // inner // 2
            put(far.at[0], 0, 2)
            put(far.at[1], half, 2)

        @pl.when(place_ref[0] == 0)
        def _():
            place(own_a, sides_a, far_a, wq_ref)
            place(own_b, sides_b, far_b, wo_ref)

        @pl.when(place_ref[0] != 0)
        def _():
            place(own_b, sides_b, far_b, wq_ref)
            place(own_a, sides_a, far_a, wo_ref)

        pooled = jnp.transpose(pt_ref[...].astype(jnp.float32))
        query_pre = dot_nn(pooled.astype(jnp.bfloat16), wq_ref[:pooled_width, :]) + dot_nn(
            dense_ref[...], wq_ref[pooled_width:, :]
        )
        gate = jax.nn.sigmoid(query_pre)
        query = (query_pre * gate).astype(jnp.bfloat16)
        query_slope = gate * (1.0 + query_pre * (1.0 - gate))

        index = lax.broadcasted_iota(jnp.int32, (cands, event_count), 1)
        owner = index % owned
        limit = jnp.full((cands, event_count), len_ref[0], jnp.int32)
        for a in range(1, owned):
            limit = jnp.where(owner == a, len_ref[a], limit)
        live = ((owner == req_ref[...]) & (index // owned < limit)).astype(jnp.float32)

        weights, slopes, attended = [], [], []
        for h in range(H):
            cols = slice(h * dim, (h + 1) * dim)
            vcols = slice(width + h * dim, width + (h + 1) * dim)
            score = dot_nt(query[:, cols], ev_ref[:, cols]) * scale
            sig = jax.nn.sigmoid(score)
            weight = (score * sig * live).astype(jnp.bfloat16)
            weights.append(weight)
            slopes.append(live * (sig * (1.0 + score * (1.0 - sig))) * scale)
            attended.append(dot_nn(weight, ev_ref[:, vcols]))
        attended = jnp.concatenate(attended, axis=1)
        centered = attended - jnp.mean(attended, axis=1, keepdims=True)
        inverse = lax.rsqrt(jnp.mean(centered * centered, axis=1, keepdims=True) + norm_eps)
        normed = centered * inverse
        mixed = dot_nn(normed.astype(jnp.bfloat16), wo_ref[...])
        out_ref[:, :pooled_width] = (mixed[:, :pooled_width] + pooled).astype(jnp.bfloat16)
        out_ref[:, pooled_width:] = (mixed[:, pooled_width:] + dense_ref[...].astype(jnp.float32)).astype(
            jnp.bfloat16
        )
        back_y = dot_nt(cot_ref[...], wo_ref[...])
        back_att = inverse * (
            back_y
            - jnp.mean(back_y, axis=1, keepdims=True)
            - normed * jnp.mean(back_y * normed, axis=1, keepdims=True)
        )
        back_att = back_att.astype(jnp.bfloat16)
        back_query = []
        for h in range(H):
            cols = slice(h * dim, (h + 1) * dim)
            vcols = slice(width + h * dim, width + (h + 1) * dim)
            back_w = dot_nt(back_att[:, cols], ev_ref[:, vcols])
            back_s = (back_w * slopes[h]).astype(jnp.bfloat16)
            back_query.append(dot_nn(back_s, ev_ref[:, cols]))
            kv_ref[:, cols] = dot_tn(back_s, query[:, cols]).astype(jnp.bfloat16)
            kv_ref[:, vcols] = dot_tn(weights[h], back_att[:, cols]).astype(jnp.bfloat16)
        back_pre = (jnp.concatenate(back_query, axis=1) * query_slope).astype(jnp.bfloat16)
        columns = dot_nt(wq_ref[:pooled_width, :], back_pre)
        pool_ref[...] = (jnp.transpose(cot_ref[:, :pooled_width].astype(jnp.float32)) + columns).astype(
            jnp.bfloat16
        )

    vmem = pl.BlockSpec(memory_space=pltpu.VMEM)
    return pl.pallas_call(
        kernel,
        in_specs=[pl.BlockSpec(memory_space=pltpu.SMEM)] * 2 + [vmem] * 11,
        out_specs=[vmem] * 3,
        out_shape=[
            jax.ShapeDtypeStruct((cands, width), jnp.bfloat16),
            jax.ShapeDtypeStruct((event_count, 2 * width), jnp.bfloat16),
            jax.ShapeDtypeStruct((pooled_width, cands), jnp.bfloat16),
        ],
        scratch_shapes=[pltpu.VMEM((width, width), jnp.bfloat16)] * 2,
        compiler_params=pltpu.CompilerParams(vmem_limit_bytes=40 << 20),
        cost_estimate=pl.CostEstimate(
            flops=8 * cands * width * width, bytes_accessed=8 * width * width, transcendentals=0
        ),
        name="layer",
    )(place_index, lengths, pooled_t, dense, cot, *mine, *other, events, requests)


def on_device(dense_feat, emb_ids, tables, history_kv, hist_len, cand_request, w_query, w_out, cotangent):
    _, emb_width, _ = tables.shape
    sizes = {a: lax.axis_size(a) for a in ALL}
    cand_devices = sizes["x"] * sizes["yl"] * sizes["core"]
    own_rows, model_width = w_query.shape
    owned, own_events, kv_width = history_kv.shape
    group = emb_ids.shape[2]
    cands = group // cand_devices

    own = jnp.concatenate([w_query, w_out], axis=0).reshape(1, 2, own_rows, model_width)
    slab = sizes["yh"] * sizes["z"] * sizes["yl"]
    own = jnp.broadcast_to(own, (slab, 2, own_rows, model_width)).reshape(2 * slab, own_rows, model_width)
    w1 = lax.all_to_all(own, ("yh", "z", "yl", "core"), 0, 0).reshape(2 * slab * own_rows, model_width)
    half = group // 2
    pooled_a = pooled_lookup(emb_ids[0, :, :half], tables[0])

    ring = sizes["x"]
    up = [(i, (i + 1) % ring) for i in range(ring)]
    down = [(i, (i - 1) % ring) for i in range(ring)]
    swap = [(0, 1), (1, 0)]
    left = lax.ppermute(w1, "x", up)
    right = lax.ppermute(w1, "x", down)
    other_own = lax.ppermute(w1, "core", swap)

    pooled_b = pooled_lookup(emb_ids[0, :, half:], tables[0])

    own = own_events * owned
    own_hist = jnp.transpose(history_kv, (1, 0, 2)).reshape(1, own, kv_width)
    sent = jnp.concatenate([pooled_a, pooled_b], axis=1).reshape(emb_width, cand_devices, cands)
    sent = jnp.transpose(sent, (1, 0, 2)).reshape(cand_devices, own, -1)
    joined = jnp.concatenate([jnp.broadcast_to(own_hist, (cand_devices, own, kv_width)), sent], axis=2)
    front = lax.all_to_all(joined, CAND, 0, 0)
    events = front[:, :, :kv_width].reshape(cand_devices * own, kv_width)
    pooled_t = front[:, :, kv_width:].reshape(-1, cands)

    middle = w1.shape[0] // 2
    far_a = lax.ppermute(left[:middle], "x", up)
    far_b = lax.ppermute(right[middle:], "x", down)
    sides = jnp.stack([left, right])
    other_sides = lax.ppermute(sides, "core", swap)
    far = jnp.stack([far_a, far_b])
    other_far = lax.ppermute(far, "core", swap)

    cand_out, kv_part, back_pool = layer(
        pooled_t,
        dense_feat,
        cotangent,
        (w1, sides, far),
        (other_own, other_sides, other_far),
        jnp.stack([lax.axis_index("core"), lax.axis_index("x")]),
        events,
        cand_request.reshape(-1, 1),
        hist_len,
    )

    joined = jnp.concatenate(
        [kv_part.reshape(cand_devices, own, kv_width), back_pool.reshape(cand_devices, own, -1)], axis=2
    )
    back = lax.all_to_all(joined, CAND, 0, 0)
    d_kv = jnp.sum(back[:, :, :kv_width].astype(jnp.float32), axis=0)
    d_kv = jnp.transpose(d_kv.reshape(own_events, owned, kv_width), (1, 0, 2))
    pool_all = back[:, :, kv_width:].reshape(cand_devices, emb_width, cands)
    d_pooled = jnp.transpose(pool_all, (1, 0, 2)).reshape(1, emb_width, group)
    return cand_out, d_kv, d_pooled


def solution(mesh):
    parts = Mesh(mesh.devices.reshape(2, 8, 4, 4, 2), ALL)
    rows = P(ALL, None)
    return jax.shard_map(
        on_device,
        mesh=parts,
        in_specs=(
            rows,
            P(CAND, None, REQ),
            P(CAND, None, None),
            P(REQ, CAND, None),
            P(REQ),
            P(ALL),
            rows,
            rows,
            rows,
        ),
        out_specs=(rows, P(REQ, CAND, None), P(CAND, None, REQ)),
        check_vma=False,
    )
```

```python
import math

import jax
import jax.numpy as jnp
from jax import lax
from jax.experimental import pallas as pl
from jax.experimental.pallas import tpu as pltpu
from jax.sharding import Mesh, PartitionSpec as P


H = 8
norm_eps = 1e-05

REQ = ("yh", "z")
CAND = ("x", "yl", "core")
ALL = REQ + CAND


LOW = 512
TILE = 256


def lookup(ids, table, history, cands):
    bag, count = ids.shape
    emb, rows = table.shape
    hist_rows, hist_width = history.shape
    highs = rows // LOW
    step = min(count, 4 * TILE)
    half = emb // 2

    def kernel(ids_ref, table_ref, history_ref, out_ref, stacked_ref):
        @pl.when(pl.program_id(0) == 0)
        def _():
            for high in range(highs):
                stacked_ref[high * emb : (high + 1) * emb, :] = table_ref[:, high * LOW : (high + 1) * LOW]

        low_iota = lax.broadcasted_iota(jnp.int32, (LOW, TILE), 0)
        for run in range(step // cands):
            out_ref[run, :, :hist_width] = history_ref[...]
        for tile in range(step // TILE):
            span = slice(tile * TILE, (tile + 1) * TILE)
            total = jnp.zeros((emb, TILE), jnp.float32)
            for slot in range(bag):
                row = ids_ref[slot : slot + 1, span]
                low = jnp.bitwise_and(row, LOW - 1)
                high_of = jnp.broadcast_to(jnp.right_shift(row, LOW.bit_length() - 1), (emb, TILE))
                one_hot = (low_iota == low).astype(jnp.float32).astype(jnp.bfloat16)
                picked = jnp.dot(stacked_ref[...], one_hot, preferred_element_type=jnp.float32)
                found = jnp.zeros((emb, TILE), jnp.float32)
                for high in range(highs):
                    found = jnp.where(high_of == high, picked[high * emb : (high + 1) * emb, :], found)
                total = total + found
            for run in range(TILE // cands):
                cols = slice(run * cands, (run + 1) * cands)
                for part in range(2):
                    first = hist_width + part * cands
                    out_ref[tile * (TILE // cands) + run, :, first : first + cands] = total[
                        part * half : (part + 1) * half, cols
                    ].astype(jnp.bfloat16)

    width = hist_width + 2 * cands
    return pl.pallas_call(
        kernel,
        grid=(count // step,),
        in_specs=[
            pl.BlockSpec((bag, step), lambda i: (0, i)),
            pl.BlockSpec((emb, rows), lambda i: (0, 0)),
            pl.BlockSpec((hist_rows, hist_width), lambda i: (0, 0)),
        ],
        out_specs=pl.BlockSpec((step // cands, hist_rows, width), lambda i: (i, 0, 0)),
        out_shape=jax.ShapeDtypeStruct((count // cands, hist_rows, width), jnp.bfloat16),
        scratch_shapes=[pltpu.VMEM((highs * emb, LOW), jnp.bfloat16)],
        compiler_params=pltpu.CompilerParams(vmem_limit_bytes=32 << 20),
        cost_estimate=pl.CostEstimate(
            flops=2 * emb * rows * bag * count, bytes_accessed=2 * emb * rows, transcendentals=0
        ),
        name="lookup",
    )(ids, table, history)


def dot_nn(left, right):
    return jnp.dot(left, right, preferred_element_type=jnp.float32)


def dot_nt(left, right):
    return lax.dot_general(left, right, (((1,), (1,)), ((), ())), preferred_element_type=jnp.float32)


def dot_tn(left, right):
    return lax.dot_general(left, right, (((0,), (0,)), ((), ())), preferred_element_type=jnp.float32)


def layer(front, dense, cot, mine, other, place_index, requests, lengths, own_events):
    cands, dense_width = dense.shape
    own_shape = mine[0].shape
    width = own_shape[1]
    pooled_width = width - dense_width
    block = own_shape[0]
    outer = width // block
    inner = 16
    dim = width // H
    row_count = front.shape[0]
    owned = lengths.shape[0]
    shift = owned * own_events
    group_rows = 2 * shift
    sources = row_count // group_rows
    scale = 1.0 / math.sqrt(dim)

    def kernel(
        place_ref, len_ref, front_ref, dense_ref, cot_hbm,
        own_a, sides_a, far_a, own_b, sides_b, far_b, req_ref,
        out_ref, back_ref, wq_ref, wo_ref, cot_ref, cot_sem,
    ):
        cot_copy = pltpu.make_async_copy(cot_hbm, cot_ref, cot_sem)
        cot_copy.start()
        x = place_ref[1]

        def place(own, sides, far, target):
            def put(source, first, offset):
                for i in range(source.shape[0] // inner):
                    start = pl.multiple_of(((first + i) * outer + lax.rem(x + offset, outer)) * inner, inner)
                    target[pl.ds(start, inner), :] = source[i * inner : (i + 1) * inner, :]

            put(own, 0, 0)
            put(sides.at[0], 0, outer - 1)
            put(sides.at[1], 0, 1)
            half = block // inner // 2
            put(far.at[0], 0, 2)
            put(far.at[1], half, 2)

        @pl.when(place_ref[0] == 0)
        def _():
            place(own_a, sides_a, far_a, wq_ref)
            place(own_b, sides_b, far_b, wo_ref)

        @pl.when(place_ref[0] != 0)
        def _():
            place(own_b, sides_b, far_b, wq_ref)
            place(own_a, sides_a, far_a, wo_ref)

        parts = [front_ref[:, width + p * cands : width + (p + 1) * cands].astype(jnp.float32) for p in range(2)]
        pooled = jnp.concatenate(
            [parts[p][t * group_rows : (t + 1) * group_rows, :] for t in range(sources) for p in range(2)], axis=0
        )
        pooled = jnp.transpose(pooled)
        query_pre = dot_nn(pooled.astype(jnp.bfloat16), wq_ref[:pooled_width, :]) + dot_nn(
            dense_ref[...], wq_ref[pooled_width:, :]
        )
        gate = jax.nn.sigmoid(query_pre)
        query = (query_pre * gate).astype(jnp.bfloat16)
        query_slope = gate * (1.0 + query_pre * (1.0 - gate))

        index = lax.broadcasted_iota(jnp.int32, (cands, row_count), 1)
        within = index % group_rows
        owner = within // own_events
        time = index // group_rows * own_events + within % own_events
        limit = jnp.full((cands, row_count), len_ref[0], jnp.int32)
        for a in range(1, owned):
            limit = jnp.where(owner == a, len_ref[a], limit)
        live = (owner == req_ref[...]) & (time < limit)

        weights, slopes, attended = [], [], []
        for h in range(H):
            cols = slice(h * dim, (h + 1) * dim)
            score = dot_nt(query[:, cols], front_ref[:, cols]) * scale
            sig = jax.nn.sigmoid(score)
            weight = jnp.where(live, score * sig, 0.0)
            weights.append(pltpu.roll(weight, shift, 1).astype(jnp.bfloat16))
            slopes.append(jnp.where(live, sig * (1.0 + score * (1.0 - sig)) * scale, 0.0))
            attended.append(dot_nn(weights[h], front_ref[:, cols]))
        attended = jnp.concatenate(attended, axis=1)
        centered = attended - jnp.mean(attended, axis=1, keepdims=True)
        inverse = lax.rsqrt(jnp.mean(centered * centered, axis=1, keepdims=True) + norm_eps)
        normed = centered * inverse
        mixed = dot_nn(normed.astype(jnp.bfloat16), wo_ref[...])
        out_ref[:, :pooled_width] = (mixed[:, :pooled_width] + pooled).astype(jnp.bfloat16)
        out_ref[:, pooled_width:] = (mixed[:, pooled_width:] + dense_ref[...].astype(jnp.float32)).astype(
            jnp.bfloat16
        )
        cot_copy.wait()
        back_y = dot_nt(cot_ref[...], wo_ref[...])
        back_att = inverse * (
            back_y
            - jnp.mean(back_y, axis=1, keepdims=True)
            - normed * jnp.mean(back_y * normed, axis=1, keepdims=True)
        )
        back_att = back_att.astype(jnp.bfloat16)
        back_query = []
        for h in range(H):
            cols = slice(h * dim, (h + 1) * dim)
            back_w = dot_nt(back_att[:, cols], front_ref[:, cols])
            back_w = pltpu.roll(back_w, row_count - shift, 1)
            back_s = (back_w * slopes[h]).astype(jnp.bfloat16)
            back_query.append(dot_nn(back_s, front_ref[:, cols]))
            back_ref[:, cols] = dot_tn(
                jnp.concatenate([back_s, weights[h]], axis=0),
                jnp.concatenate([query[:, cols], back_att[:, cols]], axis=0),
            ).astype(jnp.bfloat16)
        back_pre = (jnp.concatenate(back_query, axis=1) * query_slope).astype(jnp.bfloat16)
        pool = jnp.transpose(cot_ref[:, :pooled_width].astype(jnp.float32)) + dot_nt(
            wq_ref[:pooled_width, :], back_pre
        )
        for p in range(2):
            part = jnp.concatenate(
                [
                    pool[(2 * t + p) * group_rows : (2 * t + p + 1) * group_rows, :]
                    for t in range(sources)
                ],
                axis=0,
            )
            back_ref[:, width + p * cands : width + (p + 1) * cands] = part.astype(jnp.bfloat16)

    vmem = pl.BlockSpec(memory_space=pltpu.VMEM)
    smem = pl.BlockSpec(memory_space=pltpu.SMEM)
    hbm = pl.BlockSpec(memory_space=pltpu.HBM)
    return pl.pallas_call(
        kernel,
        in_specs=[smem, smem, vmem, vmem, hbm] + [vmem] * 7,
        out_specs=[vmem] * 2,
        out_shape=[
            jax.ShapeDtypeStruct((cands, width), jnp.bfloat16),
            jax.ShapeDtypeStruct(front.shape, jnp.bfloat16),
        ],
        scratch_shapes=[pltpu.VMEM((width, width), jnp.bfloat16)] * 2
        + [pltpu.VMEM((cands, width), jnp.bfloat16), pltpu.SemaphoreType.DMA],
        compiler_params=pltpu.CompilerParams(vmem_limit_bytes=40 << 20),
        cost_estimate=pl.CostEstimate(
            flops=8 * cands * width * width, bytes_accessed=8 * width * width, transcendentals=0
        ),
        name="layer",
    )(place_index, lengths, front, dense, cot, *mine, *other, requests)


def on_device(dense_feat, emb_ids, tables, history_kv, hist_len, cand_request, w_query, w_out, cotangent):
    _, emb_width, _ = tables.shape
    sizes = {a: lax.axis_size(a) for a in ALL}
    cand_devices = sizes["x"] * sizes["yl"] * sizes["core"]
    _, model_width = w_query.shape
    owned, own_events, _ = history_kv.shape
    group = emb_ids.shape[2]
    cands = group // cand_devices
    ring = sizes["x"]
    up = [(i, (i + 1) % ring) for i in range(ring)]
    down = [(i, (i - 1) % ring) for i in range(ring)]
    swap = [(0, 1), (1, 0)]

    first_core = lax.axis_index("core") == 0
    kept = jnp.where(first_core, w_query, w_out)
    got = lax.ppermute(jnp.where(first_core, w_out, w_query), "core", swap)
    own = jnp.concatenate([jnp.where(first_core, kept, got), jnp.where(first_core, got, kept)], axis=0)
    slab = sizes["yh"] * sizes["z"] * sizes["yl"]
    w1 = lax.all_to_all(jnp.broadcast_to(own[None], (slab,) + own.shape), ("yh", "z", "yl"), 0, 0)
    w1 = w1.reshape(-1, model_width)

    history = jnp.transpose(history_kv.reshape(owned, own_events, 2, model_width), (2, 0, 1, 3))
    history = history.reshape(-1, model_width)
    blocks = lookup(emb_ids[0], tables[0], history, cands)

    left = lax.ppermute(w1, "x", up)
    right = lax.ppermute(w1, "x", down)
    other_own = lax.ppermute(w1, "core", swap)

    front = lax.all_to_all(blocks, CAND, 0, 0)
    front = front.reshape(-1, front.shape[2])

    middle = w1.shape[0] // 2
    far_a = lax.ppermute(left[:middle], "x", up)
    far_b = lax.ppermute(right[middle:], "x", down)
    sides = jnp.stack([left, right])
    other_sides = lax.ppermute(sides, "core", swap)
    far = jnp.stack([far_a, far_b])
    other_far = lax.ppermute(far, "core", swap)

    cand_out, back = layer(
        front,
        dense_feat,
        cotangent,
        (w1, sides, far),
        (other_own, other_sides, other_far),
        jnp.stack([lax.axis_index("core"), lax.axis_index("x")]),
        cand_request.reshape(-1, 1),
        hist_len,
        own_events,
    )

    back = lax.all_to_all(back.reshape(cand_devices, -1, back.shape[1]), CAND, 0, 0)
    d_kv = jnp.sum(back[:, :, :model_width].astype(jnp.float32), axis=0)
    d_kv = jnp.transpose(d_kv.reshape(2, owned, own_events, model_width), (1, 2, 0, 3))
    d_kv = d_kv.reshape(owned, own_events, 2 * model_width)
    pool = back[:, :, model_width:].reshape(cand_devices, -1, 2, cands)
    d_pooled = jnp.transpose(pool, (2, 1, 0, 3)).reshape(1, emb_width, group)
    return cand_out, d_kv, d_pooled


def solution(mesh):
    parts = Mesh(mesh.devices.reshape(2, 8, 4, 4, 2), ALL)
    rows = P(ALL, None)
    return jax.shard_map(
        on_device,
        mesh=parts,
        in_specs=(
            rows,
            P(CAND, None, REQ),
            P(CAND, None, None),
            P(REQ, CAND, None),
            P(REQ),
            P(ALL),
            rows,
            rows,
            rows,
        ),
        out_specs=(rows, P(REQ, CAND, None), P(CAND, None, REQ)),
        check_vma=False,
    )
```

```python
import math

import jax
import jax.numpy as jnp
from jax import lax
from jax.experimental import pallas as pl
from jax.experimental.pallas import tpu as pltpu
from jax.sharding import Mesh, PartitionSpec as P


H = 8
norm_eps = 1e-05

REQ = ("yh", "z")
CAND = ("x", "yl", "core")
ALL = REQ + CAND


LOW = 512
TILE = 256


def lookup(ids, table, history, cands):
    bag, count = ids.shape
    emb, rows = table.shape
    hist_rows = history.shape[0]
    hist_width = history.shape[1] // 2
    highs = rows // LOW
    step = min(count, 4 * TILE)
    half = emb // 2

    def kernel(ids_ref, table_ref, history_ref, out_ref, stacked_ref):
        @pl.when(pl.program_id(0) == 0)
        def _():
            for high in range(highs):
                stacked_ref[high * emb : (high + 1) * emb, :] = table_ref[:, high * LOW : (high + 1) * LOW]

        low_iota = lax.broadcasted_iota(jnp.int32, (LOW, TILE), 0)
        for run in range(step // cands):
            core = run % 2
            out_ref[run, :, :hist_width] = history_ref[:, core * hist_width : (core + 1) * hist_width]
        for tile in range(step // TILE):
            span = slice(tile * TILE, (tile + 1) * TILE)
            total = jnp.zeros((emb, TILE), jnp.float32)
            for slot in range(bag):
                row = ids_ref[slot : slot + 1, span]
                low = jnp.bitwise_and(row, LOW - 1)
                high_of = jnp.broadcast_to(jnp.right_shift(row, LOW.bit_length() - 1), (emb, TILE))
                one_hot = (low_iota == low).astype(jnp.float32).astype(jnp.bfloat16)
                picked = jnp.dot(stacked_ref[...], one_hot, preferred_element_type=jnp.float32)
                found = jnp.zeros((emb, TILE), jnp.float32)
                for high in range(highs):
                    found = jnp.where(high_of == high, picked[high * emb : (high + 1) * emb, :], found)
                total = total + found
            for run in range(TILE // cands):
                cols = slice(run * cands, (run + 1) * cands)
                for part in range(2):
                    first = hist_width + part * cands
                    out_ref[tile * (TILE // cands) + run, :, first : first + cands] = total[
                        part * half : (part + 1) * half, cols
                    ].astype(jnp.bfloat16)

    width = hist_width + 2 * cands
    return pl.pallas_call(
        kernel,
        grid=(count // step,),
        in_specs=[
            pl.BlockSpec((bag, step), lambda i: (0, i)),
            pl.BlockSpec((emb, rows), lambda i: (0, 0)),
            pl.BlockSpec(history.shape, lambda i: (0, 0)),
        ],
        out_specs=pl.BlockSpec((step // cands, hist_rows, width), lambda i: (i, 0, 0)),
        out_shape=jax.ShapeDtypeStruct((count // cands, hist_rows, width), jnp.bfloat16),
        scratch_shapes=[pltpu.VMEM((highs * emb, LOW), jnp.bfloat16)],
        compiler_params=pltpu.CompilerParams(vmem_limit_bytes=32 << 20),
        cost_estimate=pl.CostEstimate(
            flops=2 * emb * rows * bag * count, bytes_accessed=2 * emb * rows, transcendentals=0
        ),
        name="lookup",
    )(ids, table, history)


def dot_nn(left, right):
    return jnp.dot(left, right, preferred_element_type=jnp.float32)


def dot_nt(left, right):
    return lax.dot_general(left, right, (((1,), (1,)), ((), ())), preferred_element_type=jnp.float32)


def dot_tn(left, right):
    return lax.dot_general(left, right, (((0,), (0,)), ((), ())), preferred_element_type=jnp.float32)


def layer(front, front_other, dense, cot, mine, other, place_index, requests, lengths, own_events):
    cands, dense_width = dense.shape
    block, width = mine[0].shape
    pooled_width = width - dense_width
    outer = width // block
    inner = 16
    dim = width // H
    row_count = front.shape[0]
    hist_width = front_other.shape[1]
    owned = lengths.shape[0]
    shift = owned * own_events
    group_rows = 2 * shift
    sources = row_count // group_rows
    scale = 1.0 / math.sqrt(dim)

    def kernel(
        place_ref, len_ref, front_ref, front_other_ref, dense_hbm, cot_hbm, req_ref, *rest
    ):
        mine_refs, other_refs = rest[:5], rest[5:10]
        out_ref, back_ref, wq_ref, wo_ref, ev_ref, cot_ref, dense_ref, cot_sem, dense_sem = rest[10:]
        cot_copy = pltpu.make_async_copy(cot_hbm, cot_ref, cot_sem)
        dense_copy = pltpu.make_async_copy(dense_hbm, dense_ref, dense_sem)
        dense_copy.start()
        cot_copy.start()
        x = place_ref[1]

        def place(pieces, target):
            half = block // inner // 2
            for piece, first, offset in zip(pieces, (0, 0, 0, 0, half), (0, outer - 1, 1, 2, 2)):
                for i in range(piece.shape[0] // inner):
                    start = pl.multiple_of(((first + i) * outer + lax.rem(x + offset, outer)) * inner, inner)
                    target[pl.ds(start, inner), :] = piece[i * inner : (i + 1) * inner, :]

        @pl.when(place_ref[0] == 0)
        def _():
            place(mine_refs, wq_ref)
            place(other_refs, wo_ref)
            ev_ref[:, :hist_width] = front_ref[:, :hist_width]
            ev_ref[:, hist_width:] = front_other_ref[...]

        @pl.when(place_ref[0] != 0)
        def _():
            place(other_refs, wq_ref)
            place(mine_refs, wo_ref)
            ev_ref[:, :hist_width] = front_other_ref[...]
            ev_ref[:, hist_width:] = front_ref[:, :hist_width]

        parts = [
            front_ref[:, hist_width + p * cands : hist_width + (p + 1) * cands].astype(jnp.float32) for p in range(2)
        ]
        pooled = jnp.concatenate(
            [parts[p][t * group_rows : (t + 1) * group_rows, :] for t in range(sources) for p in range(2)], axis=0
        )
        pooled = jnp.transpose(pooled)
        dense_copy.wait()
        query_pre = dot_nn(pooled.astype(jnp.bfloat16), wq_ref[:pooled_width, :]) + dot_nn(
            dense_ref[...], wq_ref[pooled_width:, :]
        )
        gate = jax.nn.sigmoid(query_pre)
        query = (query_pre * gate).astype(jnp.bfloat16)
        query_slope = gate * (1.0 + query_pre * (1.0 - gate))

        index = lax.broadcasted_iota(jnp.int32, (cands, row_count), 1)
        within = index % group_rows
        owner = within // own_events
        time = index // group_rows * own_events + within % own_events
        limit = jnp.full((cands, row_count), len_ref[0], jnp.int32)
        for a in range(1, owned):
            limit = jnp.where(owner == a, len_ref[a], limit)
        request = jnp.transpose(jnp.broadcast_to(req_ref[...].astype(jnp.float32), (cands, cands))).astype(jnp.int32)
        request = jnp.concatenate([request] * (row_count // cands), axis=1)
        live = (owner == request) & (time < limit)

        weights, slopes, attended = [], [], []
        for h in range(H):
            cols = slice(h * dim, (h + 1) * dim)
            score = dot_nt(query[:, cols], ev_ref[:, cols]) * scale
            sig = jax.nn.sigmoid(score)
            weight = jnp.where(live, score * sig, 0.0)
            weights.append(pltpu.roll(weight, shift, 1).astype(jnp.bfloat16))
            slopes.append(jnp.where(live, sig * (1.0 + score * (1.0 - sig)) * scale, 0.0))
            attended.append(dot_nn(weights[h], ev_ref[:, cols]))
        attended = jnp.concatenate(attended, axis=1)
        centered = attended - jnp.mean(attended, axis=1, keepdims=True)
        inverse = lax.rsqrt(jnp.mean(centered * centered, axis=1, keepdims=True) + norm_eps)
        normed = centered * inverse
        mixed = dot_nn(normed.astype(jnp.bfloat16), wo_ref[...])
        out_ref[:, :pooled_width] = (mixed[:, :pooled_width] + pooled).astype(jnp.bfloat16)
        out_ref[:, pooled_width:] = (mixed[:, pooled_width:] + dense_ref[...].astype(jnp.float32)).astype(
            jnp.bfloat16
        )
        cot_copy.wait()
        back_y = dot_nt(cot_ref[...], wo_ref[...])
        back_att = inverse * (
            back_y
            - jnp.mean(back_y, axis=1, keepdims=True)
            - normed * jnp.mean(back_y * normed, axis=1, keepdims=True)
        )
        back_att = back_att.astype(jnp.bfloat16)
        back_query = []
        for h in range(H):
            cols = slice(h * dim, (h + 1) * dim)
            back_w = dot_nt(back_att[:, cols], ev_ref[:, cols])
            back_w = pltpu.roll(back_w, row_count - shift, 1)
            back_s = (back_w * slopes[h]).astype(jnp.bfloat16)
            back_query.append(dot_nn(back_s, ev_ref[:, cols]))
            back_ref[:, cols] = dot_tn(
                jnp.concatenate([back_s, weights[h]], axis=0),
                jnp.concatenate([query[:, cols], back_att[:, cols]], axis=0),
            ).astype(jnp.bfloat16)
        back_pre = (jnp.concatenate(back_query, axis=1) * query_slope).astype(jnp.bfloat16)
        pool = jnp.transpose(cot_ref[:, :pooled_width].astype(jnp.float32)) + dot_nt(
            wq_ref[:pooled_width, :], back_pre
        )
        for p in range(2):
            part = jnp.concatenate(
                [
                    pool[(2 * t + p) * group_rows : (2 * t + p + 1) * group_rows, :]
                    for t in range(sources)
                ],
                axis=0,
            )
            back_ref[:, width + p * cands : width + (p + 1) * cands] = part.astype(jnp.bfloat16)

    vmem = pl.BlockSpec(memory_space=pltpu.VMEM)
    smem = pl.BlockSpec(memory_space=pltpu.SMEM)
    hbm = pl.BlockSpec(memory_space=pltpu.HBM)
    return pl.pallas_call(
        kernel,
        in_specs=[smem, smem, vmem, vmem, hbm, hbm] + [vmem] * 11,
        out_specs=[vmem] * 2,
        out_shape=[
            jax.ShapeDtypeStruct((cands, width), jnp.bfloat16),
            jax.ShapeDtypeStruct((row_count, width + 2 * cands), jnp.bfloat16),
        ],
        scratch_shapes=[pltpu.VMEM((width, width), jnp.bfloat16)] * 2
        + [
            pltpu.VMEM((row_count, width), jnp.bfloat16),
            pltpu.VMEM((cands, width), jnp.bfloat16),
            pltpu.VMEM((cands, dense_width), jnp.bfloat16),
            pltpu.SemaphoreType.DMA,
            pltpu.SemaphoreType.DMA,
        ],
        compiler_params=pltpu.CompilerParams(vmem_limit_bytes=40 << 20),
        cost_estimate=pl.CostEstimate(
            flops=8 * cands * width * width, bytes_accessed=8 * width * width, transcendentals=0
        ),
        name="layer",
    )(
        place_index,
        lengths,
        front,
        front_other,
        pltpu.with_memory_space_constraint(dense, pltpu.HBM),
        pltpu.with_memory_space_constraint(cot, pltpu.HBM),
        requests,
        *mine,
        *other,
    )


def on_device(dense_feat, emb_ids, tables, history_kv, hist_len, cand_request, w_query, w_out, cotangent):
    _, emb_width, _ = tables.shape
    sizes = {a: lax.axis_size(a) for a in ALL}
    cand_devices = sizes["x"] * sizes["yl"] * sizes["core"]
    own_rows, model_width = w_query.shape
    owned, own_events, _ = history_kv.shape
    group = emb_ids.shape[2]
    cands = group // cand_devices
    ring = sizes["x"]
    up = [(i, (i + 1) % ring) for i in range(ring)]
    down = [(i, (i - 1) % ring) for i in range(ring)]
    swap = [(0, 1), (1, 0)]

    own = jnp.concatenate([w_query, w_out], axis=0).reshape(1, 2, own_rows, model_width)
    slab = sizes["yh"] * sizes["z"] * sizes["yl"]
    own = jnp.broadcast_to(own, (slab, 2, own_rows, model_width)).reshape(2 * slab, own_rows, model_width)
    w1 = lax.all_to_all(own, ("yh", "z", "yl", "core"), 0, 0)
    w1 = w1.reshape(-1, model_width)

    history = jnp.transpose(history_kv.reshape(owned, own_events, 2, model_width), (2, 0, 1, 3))
    history = history.reshape(-1, model_width)
    blocks = lookup(emb_ids[0], tables[0], history, cands)

    left = lax.ppermute(w1, "x", up)
    right = lax.ppermute(w1, "x", down)
    front = lax.all_to_all(blocks, CAND, 0, 0)
    front = front.reshape(-1, front.shape[2])
    hist_width = model_width // 2
    front_other = lax.ppermute(front[:, :hist_width], "core", swap)

    middle = w1.shape[0] // 2
    far_a = lax.ppermute(left[:middle], "x", up)
    far_b = lax.ppermute(right[middle:], "x", down)
    mine = (w1, left, right, far_a, far_b)
    other = []
    for piece in mine:
        other.append(lax.ppermute(piece, "core", swap))

    cand_out, back = layer(
        front,
        front_other,
        dense_feat,
        cotangent,
        mine,
        tuple(other),
        jnp.stack([lax.axis_index("core"), lax.axis_index("x")]),
        cand_request.reshape(1, -1),
        hist_len,
        own_events,
    )

    back = lax.all_to_all(back.reshape(cand_devices, -1, back.shape[1]), CAND, 0, 0)
    d_kv = jnp.sum(back[:, :, :model_width].astype(jnp.float32), axis=0)
    d_kv = jnp.transpose(d_kv.reshape(2, owned, own_events, model_width), (1, 2, 0, 3))
    d_kv = d_kv.reshape(owned, own_events, 2 * model_width)
    pool = back[:, :, model_width:].reshape(cand_devices, -1, 2, cands)
    d_pooled = jnp.transpose(pool, (2, 1, 0, 3)).reshape(1, emb_width, group)
    return cand_out, d_kv, d_pooled


def solution(mesh):
    parts = Mesh(mesh.devices.reshape(2, 8, 4, 4, 2), ALL)
    rows = P(ALL, None)
    return jax.shard_map(
        on_device,
        mesh=parts,
        in_specs=(
            rows,
            P(CAND, None, REQ),
            P(CAND, None, None),
            P(REQ, CAND, None),
            P(REQ),
            P(ALL),
            rows,
            rows,
            rows,
        ),
        out_specs=(rows, P(REQ, CAND, None), P(CAND, None, REQ)),
        check_vma=False,
    )
```

```python
import math

import jax
import jax.numpy as jnp
from jax import lax
from jax.experimental import pallas as pl
from jax.experimental.pallas import tpu as pltpu
from jax.sharding import Mesh, PartitionSpec as P


H = 8
norm_eps = 1e-05

REQ = ("yh", "z")
CAND = ("x", "yl", "core")
ALL = REQ + CAND


LOW = 512
TILE = 256


def lookup(ids, table, history, cands):
    bag, count = ids.shape
    emb, rows = table.shape
    hist_rows = history.shape[0]
    hist_width = history.shape[1] // 2
    highs = rows // LOW
    step = min(count, 4 * TILE)
    half = emb // 2

    def kernel(ids_ref, table_ref, history_ref, out_ref, stacked_ref):
        @pl.when(pl.program_id(0) == 0)
        def _():
            for high in range(highs):
                stacked_ref[high * emb : (high + 1) * emb, :] = table_ref[:, high * LOW : (high + 1) * LOW]

        low_iota = lax.broadcasted_iota(jnp.int32, (LOW, TILE), 0)
        for run in range(step // cands):
            core = run % 2
            out_ref[run, :, :hist_width] = history_ref[:, core * hist_width : (core + 1) * hist_width]
        for tile in range(step // TILE):
            span = slice(tile * TILE, (tile + 1) * TILE)
            total = jnp.zeros((emb, TILE), jnp.float32)
            for slot in range(bag):
                row = ids_ref[slot : slot + 1, span]
                low = jnp.bitwise_and(row, LOW - 1)
                high_of = jnp.broadcast_to(jnp.right_shift(row, LOW.bit_length() - 1), (emb, TILE))
                one_hot = (low_iota == low).astype(jnp.float32).astype(jnp.bfloat16)
                picked = jnp.dot(stacked_ref[...], one_hot, preferred_element_type=jnp.float32)
                found = jnp.zeros((emb, TILE), jnp.float32)
                for high in range(highs):
                    found = jnp.where(high_of == high, picked[high * emb : (high + 1) * emb, :], found)
                total = total + found
            for run in range(TILE // cands):
                cols = slice(run * cands, (run + 1) * cands)
                for part in range(2):
                    first = hist_width + part * cands
                    out_ref[tile * (TILE // cands) + run, :, first : first + cands] = total[
                        part * half : (part + 1) * half, cols
                    ].astype(jnp.bfloat16)

    width = hist_width + 2 * cands
    return pl.pallas_call(
        kernel,
        grid=(count // step,),
        in_specs=[
            pl.BlockSpec((bag, step), lambda i: (0, i)),
            pl.BlockSpec((emb, rows), lambda i: (0, 0)),
            pl.BlockSpec(history.shape, lambda i: (0, 0)),
        ],
        out_specs=pl.BlockSpec((step // cands, hist_rows, width), lambda i: (i, 0, 0)),
        out_shape=jax.ShapeDtypeStruct((count // cands, hist_rows, width), jnp.bfloat16),
        scratch_shapes=[pltpu.VMEM((highs * emb, LOW), jnp.bfloat16)],
        compiler_params=pltpu.CompilerParams(vmem_limit_bytes=32 << 20),
        cost_estimate=pl.CostEstimate(
            flops=2 * emb * rows * bag * count, bytes_accessed=2 * emb * rows, transcendentals=0
        ),
        name="lookup",
    )(ids, table, history)


def dot_nn(left, right):
    return jnp.dot(left, right, preferred_element_type=jnp.float32)


def dot_nt(left, right):
    return lax.dot_general(left, right, (((1,), (1,)), ((), ())), preferred_element_type=jnp.float32)


def dot_tn(left, right):
    return lax.dot_general(left, right, (((0,), (0,)), ((), ())), preferred_element_type=jnp.float32)


def layer(front, front_other, dense, cot, mine, other, place_index, requests, lengths, own_events):
    cands, dense_width = dense.shape
    block, width = mine[0].shape
    pooled_width = width - dense_width
    outer = width // block
    inner = 16
    dim = width // H
    row_count = front.shape[0]
    hist_width = front_other.shape[1]
    owned = lengths.shape[0]
    shift = owned * own_events
    group_rows = 2 * shift
    sources = row_count // group_rows
    scale = 1.0 / math.sqrt(dim)

    def kernel(
        place_ref, len_ref, front_ref, front_other_ref, dense_hbm, cot_hbm, req_ref, *rest
    ):
        mine_refs, other_refs = rest[:4], rest[4:8]
        out_ref, back_ref, wq_ref, wo_ref, ev_ref, cot_ref, dense_ref, cot_sem, dense_sem = rest[8:]
        cot_copy = pltpu.make_async_copy(cot_hbm, cot_ref, cot_sem)
        dense_copy = pltpu.make_async_copy(dense_hbm, dense_ref, dense_sem)
        dense_copy.start()
        cot_copy.start()
        x = place_ref[1]

        def place(pieces, target):
            for piece, offset in zip(pieces, (0, outer - 1, 1, 2)):
                for i in range(block // inner):
                    start = pl.multiple_of((i * outer + lax.rem(x + offset, outer)) * inner, inner)
                    target[pl.ds(start, inner), :] = piece[i * inner : (i + 1) * inner, :]

        @pl.when(place_ref[0] == 0)
        def _():
            place(mine_refs, wq_ref)
            place(other_refs, wo_ref)
            ev_ref[:, :hist_width] = front_ref[:, :hist_width]
            ev_ref[:, hist_width:] = front_other_ref[...]

        @pl.when(place_ref[0] != 0)
        def _():
            place(other_refs, wq_ref)
            place(mine_refs, wo_ref)
            ev_ref[:, :hist_width] = front_other_ref[...]
            ev_ref[:, hist_width:] = front_ref[:, :hist_width]

        parts = [
            front_ref[:, hist_width + p * cands : hist_width + (p + 1) * cands].astype(jnp.float32) for p in range(2)
        ]
        pooled = jnp.concatenate(
            [parts[p][t * group_rows : (t + 1) * group_rows, :] for t in range(sources) for p in range(2)], axis=0
        )
        pooled = jnp.transpose(pooled)
        dense_copy.wait()
        query_pre = dot_nn(pooled.astype(jnp.bfloat16), wq_ref[:pooled_width, :]) + dot_nn(
            dense_ref[...], wq_ref[pooled_width:, :]
        )
        gate = jax.nn.sigmoid(query_pre)
        query = (query_pre * gate).astype(jnp.bfloat16)
        query_slope = gate * (1.0 + query_pre * (1.0 - gate))

        index = lax.broadcasted_iota(jnp.int32, (cands, row_count), 1)
        within = index % group_rows
        owner = within // own_events
        time = index // group_rows * own_events + within % own_events
        limit = jnp.full((cands, row_count), len_ref[0], jnp.int32)
        for a in range(1, owned):
            limit = jnp.where(owner == a, len_ref[a], limit)
        request = jnp.transpose(jnp.broadcast_to(req_ref[...].astype(jnp.float32), (cands, cands))).astype(jnp.int32)
        request = jnp.concatenate([request] * (row_count // cands), axis=1)
        live = (owner == request) & (time < limit)

        weights, slopes, attended = [], [], []
        for h in range(H):
            cols = slice(h * dim, (h + 1) * dim)
            score = dot_nt(query[:, cols], ev_ref[:, cols]) * scale
            sig = jax.nn.sigmoid(score)
            weight = jnp.where(live, score * sig, 0.0)
            weights.append(pltpu.roll(weight, shift, 1).astype(jnp.bfloat16))
            slopes.append(jnp.where(live, sig * (1.0 + score * (1.0 - sig)) * scale, 0.0))
            attended.append(dot_nn(weights[h], ev_ref[:, cols]))
        attended = jnp.concatenate(attended, axis=1)
        centered = attended - jnp.mean(attended, axis=1, keepdims=True)
        inverse = lax.rsqrt(jnp.mean(centered * centered, axis=1, keepdims=True) + norm_eps)
        normed = centered * inverse
        mixed = dot_nn(normed.astype(jnp.bfloat16), wo_ref[...])
        out_ref[:, :pooled_width] = (mixed[:, :pooled_width] + pooled).astype(jnp.bfloat16)
        out_ref[:, pooled_width:] = (mixed[:, pooled_width:] + dense_ref[...].astype(jnp.float32)).astype(
            jnp.bfloat16
        )
        cot_copy.wait()
        back_y = dot_nt(cot_ref[...], wo_ref[...])
        back_att = inverse * (
            back_y
            - jnp.mean(back_y, axis=1, keepdims=True)
            - normed * jnp.mean(back_y * normed, axis=1, keepdims=True)
        )
        back_att = back_att.astype(jnp.bfloat16)
        back_query = []
        for h in range(H):
            cols = slice(h * dim, (h + 1) * dim)
            back_w = dot_nt(back_att[:, cols], ev_ref[:, cols])
            back_w = pltpu.roll(back_w, row_count - shift, 1)
            back_s = (back_w * slopes[h]).astype(jnp.bfloat16)
            back_query.append(dot_nn(back_s, ev_ref[:, cols]))
            back_ref[:, cols] = dot_tn(
                jnp.concatenate([back_s, weights[h]], axis=0),
                jnp.concatenate([query[:, cols], back_att[:, cols]], axis=0),
            ).astype(jnp.bfloat16)
        back_pre = (jnp.concatenate(back_query, axis=1) * query_slope).astype(jnp.bfloat16)
        pool = jnp.transpose(cot_ref[:, :pooled_width].astype(jnp.float32)) + dot_nt(
            wq_ref[:pooled_width, :], back_pre
        )
        for p in range(2):
            part = jnp.concatenate(
                [
                    pool[(2 * t + p) * group_rows : (2 * t + p + 1) * group_rows, :]
                    for t in range(sources)
                ],
                axis=0,
            )
            back_ref[:, width + p * cands : width + (p + 1) * cands] = part.astype(jnp.bfloat16)

    vmem = pl.BlockSpec(memory_space=pltpu.VMEM)
    smem = pl.BlockSpec(memory_space=pltpu.SMEM)
    hbm = pl.BlockSpec(memory_space=pltpu.HBM)
    return pl.pallas_call(
        kernel,
        in_specs=[smem, smem, vmem, vmem, hbm, hbm] + [vmem] * 9,
        out_specs=[vmem] * 2,
        out_shape=[
            jax.ShapeDtypeStruct((cands, width), jnp.bfloat16),
            jax.ShapeDtypeStruct((row_count, width + 2 * cands), jnp.bfloat16),
        ],
        scratch_shapes=[pltpu.VMEM((width, width), jnp.bfloat16)] * 2
        + [
            pltpu.VMEM((row_count, width), jnp.bfloat16),
            pltpu.VMEM((cands, width), jnp.bfloat16),
            pltpu.VMEM((cands, dense_width), jnp.bfloat16),
            pltpu.SemaphoreType.DMA,
            pltpu.SemaphoreType.DMA,
        ],
        compiler_params=pltpu.CompilerParams(vmem_limit_bytes=40 << 20),
        cost_estimate=pl.CostEstimate(
            flops=8 * cands * width * width, bytes_accessed=8 * width * width, transcendentals=0
        ),
        name="layer",
    )(
        place_index,
        lengths,
        front,
        front_other,
        pltpu.with_memory_space_constraint(dense, pltpu.HBM),
        pltpu.with_memory_space_constraint(cot, pltpu.HBM),
        requests,
        *mine,
        *other,
    )


def on_device(dense_feat, emb_ids, tables, history_kv, hist_len, cand_request, w_query, w_out, cotangent):
    _, emb_width, _ = tables.shape
    sizes = {a: lax.axis_size(a) for a in ALL}
    cand_devices = sizes["x"] * sizes["yl"] * sizes["core"]
    own_rows, model_width = w_query.shape
    owned, own_events, _ = history_kv.shape
    group = emb_ids.shape[2]
    cands = group // cand_devices
    ring = sizes["x"]
    up = [(i, (i + 1) % ring) for i in range(ring)]
    down = [(i, (i - 1) % ring) for i in range(ring)]
    swap = [(0, 1), (1, 0)]

    own = jnp.concatenate([w_query, w_out], axis=0).reshape(1, 2, own_rows, model_width)
    slab = sizes["yh"] * sizes["z"] * sizes["yl"]
    own = jnp.broadcast_to(own, (slab, 2, own_rows, model_width)).reshape(2 * slab, own_rows, model_width)
    w1 = lax.all_to_all(own, ("yh", "z", "yl", "core"), 0, 0)
    w1 = w1.reshape(-1, model_width)

    history = jnp.transpose(history_kv.reshape(owned, own_events, 2, model_width), (2, 0, 1, 3))
    history = history.reshape(-1, model_width)
    blocks = lookup(emb_ids[0], tables[0], history, cands)

    left = lax.ppermute(w1, "x", up)
    right = lax.ppermute(w1, "x", down)
    front = lax.all_to_all(blocks, CAND, 0, 0)
    front = front.reshape(-1, front.shape[2])
    hist_width = model_width // 2
    front_other = lax.ppermute(front[:, :hist_width], "core", swap)

    both_ways = [(2 * i, 2 * ((i + 1) % ring)) for i in range(ring)] + [
        (2 * i + 1, 2 * ((i - 1) % ring) + 1) for i in range(ring)
    ]
    passed = jnp.where(lax.axis_index("core") == 0, left, right)
    far = lax.ppermute(passed, ("x", "core"), both_ways)
    mine = (w1, left, right, far)
    other = []
    for piece in mine:
        other.append(lax.ppermute(piece, "core", swap))

    cand_out, back = layer(
        front,
        front_other,
        dense_feat,
        cotangent,
        mine,
        tuple(other),
        jnp.stack([lax.axis_index("core"), lax.axis_index("x")]),
        cand_request.reshape(1, -1),
        hist_len,
        own_events,
    )

    back = lax.all_to_all(back.reshape(cand_devices, -1, back.shape[1]), CAND, 0, 0)
    d_kv = jnp.sum(back[:, :, :model_width].astype(jnp.float32), axis=0)
    d_kv = jnp.transpose(d_kv.reshape(2, owned, own_events, model_width), (1, 2, 0, 3))
    d_kv = d_kv.reshape(owned, own_events, 2 * model_width)
    pool = back[:, :, model_width:].reshape(cand_devices, -1, 2, cands)
    d_pooled = jnp.transpose(pool, (2, 1, 0, 3)).reshape(1, emb_width, group)
    return cand_out, d_kv, d_pooled


def solution(mesh):
    parts = Mesh(mesh.devices.reshape(2, 8, 4, 4, 2), ALL)
    rows = P(ALL, None)
    return jax.shard_map(
        on_device,
        mesh=parts,
        in_specs=(
            rows,
            P(CAND, None, REQ),
            P(CAND, None, None),
            P(REQ, CAND, None),
            P(REQ),
            P(ALL),
            rows,
            rows,
            rows,
        ),
        out_specs=(rows, P(REQ, CAND, None), P(CAND, None, REQ)),
        check_vma=False,
    )
```

```python
import math

import jax
import jax.numpy as jnp
from jax import lax
from jax.experimental import pallas as pl
from jax.experimental.pallas import tpu as pltpu
from jax.sharding import Mesh, PartitionSpec as P


H = 8
norm_eps = 1e-05

REQ = ("yh", "z")
CAND = ("x", "yl", "core")
ALL = REQ + CAND


LOW = 512
TILE = 256


def lookup(ids, table, history, cands, first, count, into=None):
    bag, total_count = ids.shape
    emb, rows = table.shape
    hist_rows = history.shape[0]
    hist_width = history.shape[1] // 2
    highs = rows // LOW
    step = min(count, 4 * TILE)
    half = emb // 2

    def kernel(ids_hbm, table_ref, history_ref, *rest):
        out_ref, stacked_ref, ids_ref, ids_sem = rest[-4:]

        @pl.when(pl.program_id(0) == 0)
        def _():
            ids_copy = pltpu.make_async_copy(ids_hbm.at[:, pl.ds(first, count)], ids_ref, ids_sem)
            ids_copy.start()
            for high in range(highs):
                stacked_ref[high * emb : (high + 1) * emb, :] = table_ref[:, high * LOW : (high + 1) * LOW]
            ids_copy.wait()

        offset = pl.program_id(0) * step
        low_iota = lax.broadcasted_iota(jnp.int32, (LOW, TILE), 0)
        for run in range(step // cands):
            core = run % 2
            out_ref[run, :, :hist_width] = history_ref[:, core * hist_width : (core + 1) * hist_width]
        for tile in range(step // TILE):
            span = pl.ds(pl.multiple_of(offset + tile * TILE, TILE), TILE)
            total = jnp.zeros((emb, TILE), jnp.float32)
            for slot in range(bag):
                row = ids_ref[slot : slot + 1, span]
                low = jnp.bitwise_and(row, LOW - 1)
                high_of = jnp.broadcast_to(jnp.right_shift(row, LOW.bit_length() - 1), (emb, TILE))
                one_hot = (low_iota == low).astype(jnp.float32).astype(jnp.bfloat16)
                picked = jnp.dot(stacked_ref[...], one_hot, preferred_element_type=jnp.float32)
                found = jnp.zeros((emb, TILE), jnp.float32)
                for high in range(highs):
                    found = jnp.where(high_of == high, picked[high * emb : (high + 1) * emb, :], found)
                total = total + found
            for run in range(TILE // cands):
                cols = slice(run * cands, (run + 1) * cands)
                for part in range(2):
                    column = hist_width + part * cands
                    out_ref[tile * (TILE // cands) + run, :, column : column + cands] = total[
                        part * half : (part + 1) * half, cols
                    ].astype(jnp.bfloat16)

    width = hist_width + 2 * cands
    hbm = pl.BlockSpec(memory_space=pltpu.HBM)
    arguments = (pltpu.with_memory_space_constraint(ids, pltpu.HBM), table, history)
    return pl.pallas_call(
        kernel,
        grid=(count // step,),
        in_specs=[
            hbm,
            pl.BlockSpec((emb, rows), lambda i: (0, 0)),
            pl.BlockSpec(history.shape, lambda i: (0, 0)),
        ]
        + ([] if into is None else [hbm]),
        out_specs=pl.BlockSpec((step // cands, hist_rows, width), lambda i: (first // step + i, 0, 0)),
        out_shape=jax.ShapeDtypeStruct((total_count // cands, hist_rows, width), jnp.bfloat16),
        input_output_aliases={} if into is None else {3: 0},
        scratch_shapes=[
            pltpu.VMEM((highs * emb, LOW), jnp.bfloat16),
            pltpu.VMEM((bag, count), jnp.int32),
            pltpu.SemaphoreType.DMA,
        ],
        compiler_params=pltpu.CompilerParams(vmem_limit_bytes=32 << 20),
        cost_estimate=pl.CostEstimate(
            flops=2 * emb * rows * bag * count, bytes_accessed=2 * emb * rows, transcendentals=0
        ),
        name="lookup",
    )(*arguments, *(() if into is None else (into,)))


def dot_nn(left, right):
    return jnp.dot(left, right, preferred_element_type=jnp.float32)


def dot_nt(left, right):
    return lax.dot_general(left, right, (((1,), (1,)), ((), ())), preferred_element_type=jnp.float32)


def dot_tn(left, right):
    return lax.dot_general(left, right, (((0,), (0,)), ((), ())), preferred_element_type=jnp.float32)


def layer(front, front_other, dense, cot, mine, other, place_index, requests, lengths, own_events):
    cands, dense_width = dense.shape
    block, width = mine[0].shape
    pooled_width = width - dense_width
    outer = width // block
    inner = 16
    dim = width // H
    row_count = front.shape[0]
    hist_width = front_other.shape[1]
    owned = lengths.shape[0]
    shift = owned * own_events
    group_rows = 2 * shift
    sources = row_count // group_rows
    scale = 1.0 / math.sqrt(dim)

    def kernel(
        place_ref, len_ref, front_ref, front_other_ref, dense_hbm, cot_hbm, req_ref, *rest
    ):
        mine_refs, other_refs = rest[:4], rest[4:8]
        out_ref, back_ref, wq_ref, wo_ref, ev_ref, cot_ref, dense_ref, cot_sem, dense_sem = rest[8:]
        cot_copy = pltpu.make_async_copy(cot_hbm, cot_ref, cot_sem)
        dense_copy = pltpu.make_async_copy(dense_hbm, dense_ref, dense_sem)
        dense_copy.start()
        cot_copy.start()
        x = place_ref[1]

        def place(pieces, target):
            for piece, offset in zip(pieces, (0, outer - 1, 1, 2)):
                for i in range(block // inner):
                    start = pl.multiple_of((i * outer + lax.rem(x + offset, outer)) * inner, inner)
                    target[pl.ds(start, inner), :] = piece[i * inner : (i + 1) * inner, :]

        @pl.when(place_ref[0] == 0)
        def _():
            place(mine_refs, wq_ref)
            place(other_refs, wo_ref)
            ev_ref[:, :hist_width] = front_ref[:, :hist_width]
            ev_ref[:, hist_width:] = front_other_ref[...]

        @pl.when(place_ref[0] != 0)
        def _():
            place(other_refs, wq_ref)
            place(mine_refs, wo_ref)
            ev_ref[:, :hist_width] = front_other_ref[...]
            ev_ref[:, hist_width:] = front_ref[:, :hist_width]

        parts = [
            front_ref[:, hist_width + p * cands : hist_width + (p + 1) * cands].astype(jnp.float32) for p in range(2)
        ]
        pooled = jnp.concatenate(
            [parts[p][t * group_rows : (t + 1) * group_rows, :] for t in range(sources) for p in range(2)], axis=0
        )
        pooled = jnp.transpose(pooled)
        dense_copy.wait()
        query_pre = dot_nn(pooled.astype(jnp.bfloat16), wq_ref[:pooled_width, :]) + dot_nn(
            dense_ref[...], wq_ref[pooled_width:, :]
        )
        gate = jax.nn.sigmoid(query_pre)
        query = (query_pre * gate).astype(jnp.bfloat16)
        query_slope = gate * (1.0 + query_pre * (1.0 - gate))

        index = lax.broadcasted_iota(jnp.int32, (cands, row_count), 1)
        within = index % group_rows
        owner = within // own_events
        time = index // group_rows * own_events + within % own_events
        limit = jnp.full((cands, row_count), len_ref[0], jnp.int32)
        for a in range(1, owned):
            limit = jnp.where(owner == a, len_ref[a], limit)
        request = jnp.transpose(jnp.broadcast_to(req_ref[...].astype(jnp.float32), (cands, cands))).astype(jnp.int32)
        request = jnp.concatenate([request] * (row_count // cands), axis=1)
        live = (owner == request) & (time < limit)

        weights, slopes, attended = [], [], []
        for h in range(H):
            cols = slice(h * dim, (h + 1) * dim)
            score = dot_nt(query[:, cols], ev_ref[:, cols]) * scale
            sig = jax.nn.sigmoid(score)
            weight = jnp.where(live, score * sig, 0.0)
            weights.append(pltpu.roll(weight, shift, 1).astype(jnp.bfloat16))
            slopes.append(jnp.where(live, sig * (1.0 + score * (1.0 - sig)) * scale, 0.0))
            attended.append(dot_nn(weights[h], ev_ref[:, cols]))
        attended = jnp.concatenate(attended, axis=1)
        centered = attended - jnp.mean(attended, axis=1, keepdims=True)
        inverse = lax.rsqrt(jnp.mean(centered * centered, axis=1, keepdims=True) + norm_eps)
        normed = centered * inverse
        mixed = dot_nn(normed.astype(jnp.bfloat16), wo_ref[...])
        out_ref[:, :pooled_width] = (mixed[:, :pooled_width] + pooled).astype(jnp.bfloat16)
        out_ref[:, pooled_width:] = (mixed[:, pooled_width:] + dense_ref[...].astype(jnp.float32)).astype(
            jnp.bfloat16
        )
        cot_copy.wait()
        back_y = dot_nt(cot_ref[...], wo_ref[...])
        back_att = inverse * (
            back_y
            - jnp.mean(back_y, axis=1, keepdims=True)
            - normed * jnp.mean(back_y * normed, axis=1, keepdims=True)
        )
        back_att = back_att.astype(jnp.bfloat16)
        back_query = []
        for h in range(H):
            cols = slice(h * dim, (h + 1) * dim)
            back_w = dot_nt(back_att[:, cols], ev_ref[:, cols])
            back_w = pltpu.roll(back_w, row_count - shift, 1)
            back_s = (back_w * slopes[h]).astype(jnp.bfloat16)
            back_query.append(dot_nn(back_s, ev_ref[:, cols]))
            back_ref[:, cols] = dot_tn(
                jnp.concatenate([back_s, weights[h]], axis=0),
                jnp.concatenate([query[:, cols], back_att[:, cols]], axis=0),
            ).astype(jnp.bfloat16)
        back_pre = (jnp.concatenate(back_query, axis=1) * query_slope).astype(jnp.bfloat16)
        pool = jnp.transpose(cot_ref[:, :pooled_width].astype(jnp.float32)) + dot_nt(
            wq_ref[:pooled_width, :], back_pre
        )
        for p in range(2):
            part = jnp.concatenate(
                [
                    pool[(2 * t + p) * group_rows : (2 * t + p + 1) * group_rows, :]
                    for t in range(sources)
                ],
                axis=0,
            )
            back_ref[:, width + p * cands : width + (p + 1) * cands] = part.astype(jnp.bfloat16)

    vmem = pl.BlockSpec(memory_space=pltpu.VMEM)
    smem = pl.BlockSpec(memory_space=pltpu.SMEM)
    hbm = pl.BlockSpec(memory_space=pltpu.HBM)
    return pl.pallas_call(
        kernel,
        in_specs=[smem, smem, vmem, vmem, hbm, hbm] + [vmem] * 9,
        out_specs=[vmem] * 2,
        out_shape=[
            jax.ShapeDtypeStruct((cands, width), jnp.bfloat16),
            jax.ShapeDtypeStruct((row_count, width + 2 * cands), jnp.bfloat16),
        ],
        scratch_shapes=[pltpu.VMEM((width, width), jnp.bfloat16)] * 2
        + [
            pltpu.VMEM((row_count, width), jnp.bfloat16),
            pltpu.VMEM((cands, width), jnp.bfloat16),
            pltpu.VMEM((cands, dense_width), jnp.bfloat16),
            pltpu.SemaphoreType.DMA,
            pltpu.SemaphoreType.DMA,
        ],
        compiler_params=pltpu.CompilerParams(vmem_limit_bytes=40 << 20),
        cost_estimate=pl.CostEstimate(
            flops=8 * cands * width * width, bytes_accessed=8 * width * width, transcendentals=0
        ),
        name="layer",
    )(
        place_index,
        lengths,
        front,
        front_other,
        pltpu.with_memory_space_constraint(dense, pltpu.HBM),
        pltpu.with_memory_space_constraint(cot, pltpu.HBM),
        requests,
        *mine,
        *other,
    )


def on_device(dense_feat, emb_ids, tables, history_kv, hist_len, cand_request, w_query, w_out, cotangent):
    _, emb_width, _ = tables.shape
    sizes = {a: lax.axis_size(a) for a in ALL}
    cand_devices = sizes["x"] * sizes["yl"] * sizes["core"]
    own_rows, model_width = w_query.shape
    owned, own_events, _ = history_kv.shape
    group = emb_ids.shape[2]
    cands = group // cand_devices
    ring = sizes["x"]
    up = [(i, (i + 1) % ring) for i in range(ring)]
    down = [(i, (i - 1) % ring) for i in range(ring)]
    swap = [(0, 1), (1, 0)]

    slab = sizes["yh"] * sizes["z"] * sizes["yl"]
    to_core = lax.broadcasted_iota(jnp.int32, (2 * slab, own_rows, model_width), 0) % 2
    own = jnp.where(to_core == 0, w_query[None], w_out[None])
    w1 = lax.all_to_all(own, ("yh", "z", "yl", "core"), 0, 0)
    w1 = w1.reshape(-1, model_width)

    history = jnp.transpose(history_kv.reshape(owned, own_events, 2, model_width), (2, 0, 1, 3))
    history = history.reshape(-1, model_width)
    early = group // 4 * 3
    blocks = lookup(emb_ids[0], tables[0], history, cands, 0, early)

    left = lax.ppermute(w1, "x", up)
    right = lax.ppermute(w1, "x", down)
    blocks = lookup(emb_ids[0], tables[0], history, cands, early, group - early, blocks)

    front = lax.all_to_all(blocks, CAND, 0, 0)
    front = front.reshape(-1, front.shape[2])
    hist_width = model_width // 2
    front_other = lax.ppermute(front[:, :hist_width], "core", swap)

    both_ways = [(2 * i, 2 * ((i + 1) % ring)) for i in range(ring)] + [
        (2 * i + 1, 2 * ((i - 1) % ring) + 1) for i in range(ring)
    ]
    passed = jnp.where(lax.axis_index("core") == 0, left, right)
    far = lax.ppermute(passed, ("x", "core"), both_ways)
    mine = (w1, left, right, far)
    other = []
    for piece in mine:
        other.append(lax.ppermute(piece, "core", swap))

    cand_out, back = layer(
        front,
        front_other,
        dense_feat,
        cotangent,
        mine,
        tuple(other),
        jnp.stack([lax.axis_index("core"), lax.axis_index("x")]),
        cand_request.reshape(1, -1),
        hist_len,
        own_events,
    )

    back = lax.all_to_all(back.reshape(cand_devices, -1, back.shape[1]), CAND, 0, 0)
    d_kv = jnp.sum(back[:, :, :model_width].astype(jnp.float32), axis=0)
    d_kv = jnp.transpose(d_kv.reshape(2, owned, own_events, model_width), (1, 2, 0, 3))
    d_kv = d_kv.reshape(owned, own_events, 2 * model_width)
    pool = back[:, :, model_width:].reshape(cand_devices, -1, 2, cands)
    d_pooled = jnp.transpose(pool, (2, 1, 0, 3)).reshape(1, emb_width, group)
    return cand_out, d_kv, d_pooled


def solution(mesh):
    parts = Mesh(mesh.devices.reshape(2, 8, 4, 4, 2), ALL)
    rows = P(ALL, None)
    return jax.shard_map(
        on_device,
        mesh=parts,
        in_specs=(
            rows,
            P(CAND, None, REQ),
            P(CAND, None, None),
            P(REQ, CAND, None),
            P(REQ),
            P(ALL),
            rows,
            rows,
            rows,
        ),
        out_specs=(rows, P(REQ, CAND, None), P(CAND, None, REQ)),
        check_vma=False,
    )
```

```python
import math

import jax
import jax.numpy as jnp
from jax import lax
from jax.experimental import pallas as pl
from jax.experimental.pallas import tpu as pltpu
from jax.sharding import Mesh, PartitionSpec as P


H = 8
norm_eps = 1e-05

REQ = ("yh", "z")
CAND = ("x", "yl", "core")
ALL = REQ + CAND


LOW = 512
TILE = 256


def lookup(ids, table, history, cands, first, count, into=None):
    bag, total_count = ids.shape
    emb, rows = table.shape
    hist_rows = history.shape[0]
    hist_width = history.shape[1] // 2
    highs = rows // LOW
    step = min(count, 2 * TILE)
    half = emb // 2

    def kernel(ids_hbm, table_ref, history_ref, *rest):
        out_ref, stacked_ref, ids_ref, ids_sem = rest[-4:]

        @pl.when(pl.program_id(0) == 0)
        def _():
            ids_copy = pltpu.make_async_copy(ids_hbm.at[:, pl.ds(first, count)], ids_ref, ids_sem)
            ids_copy.start()
            for high in range(highs):
                stacked_ref[high * emb : (high + 1) * emb, :] = table_ref[:, high * LOW : (high + 1) * LOW]
            ids_copy.wait()

        offset = pl.program_id(0) * step
        low_iota = lax.broadcasted_iota(jnp.int32, (LOW, TILE), 0)
        for run in range(step // cands):
            core = run % 2
            out_ref[run, :, :hist_width] = history_ref[:, core * hist_width : (core + 1) * hist_width]
        for tile in range(step // TILE):
            span = pl.ds(pl.multiple_of(offset + tile * TILE, TILE), TILE)
            total = jnp.zeros((emb, TILE), jnp.float32)
            for slot in range(bag):
                row = ids_ref[slot : slot + 1, span]
                low = jnp.bitwise_and(row, LOW - 1)
                high_of = jnp.broadcast_to(jnp.right_shift(row, LOW.bit_length() - 1), (emb, TILE))
                one_hot = (low_iota == low).astype(jnp.float32).astype(jnp.bfloat16)
                picked = jnp.dot(stacked_ref[...], one_hot, preferred_element_type=jnp.float32)
                found = jnp.zeros((emb, TILE), jnp.float32)
                for high in range(highs):
                    found = jnp.where(high_of == high, picked[high * emb : (high + 1) * emb, :], found)
                total = total + found
            for run in range(TILE // cands):
                cols = slice(run * cands, (run + 1) * cands)
                for part in range(2):
                    column = hist_width + part * cands
                    out_ref[tile * (TILE // cands) + run, :, column : column + cands] = total[
                        part * half : (part + 1) * half, cols
                    ].astype(jnp.bfloat16)

    width = hist_width + 2 * cands
    hbm = pl.BlockSpec(memory_space=pltpu.HBM)
    arguments = (pltpu.with_memory_space_constraint(ids, pltpu.HBM), table, history)
    return pl.pallas_call(
        kernel,
        grid=(count // step,),
        in_specs=[
            hbm,
            pl.BlockSpec((emb, rows), lambda i: (0, 0)),
            pl.BlockSpec(history.shape, lambda i: (0, 0)),
        ]
        + ([] if into is None else [hbm]),
        out_specs=pl.BlockSpec((step // cands, hist_rows, width), lambda i: (first // step + i, 0, 0)),
        out_shape=jax.ShapeDtypeStruct((total_count // cands, hist_rows, width), jnp.bfloat16),
        input_output_aliases={} if into is None else {3: 0},
        scratch_shapes=[
            pltpu.VMEM((highs * emb, LOW), jnp.bfloat16),
            pltpu.VMEM((bag, count), jnp.int32),
            pltpu.SemaphoreType.DMA,
        ],
        compiler_params=pltpu.CompilerParams(vmem_limit_bytes=32 << 20),
        cost_estimate=pl.CostEstimate(
            flops=2 * emb * rows * bag * count, bytes_accessed=2 * emb * rows, transcendentals=0
        ),
        name="lookup",
    )(*arguments, *(() if into is None else (into,)))


def dot_nn(left, right):
    return jnp.dot(left, right, preferred_element_type=jnp.float32)


def dot_nt(left, right):
    return lax.dot_general(left, right, (((1,), (1,)), ((), ())), preferred_element_type=jnp.float32)


def dot_tn(left, right):
    return lax.dot_general(left, right, (((0,), (0,)), ((), ())), preferred_element_type=jnp.float32)


def layer(front, front_other, dense, cot, mine, other, place_index, requests, lengths, own_events):
    cands, dense_width = dense.shape
    block, width = mine[1].shape
    pooled_width = width - dense_width
    outer = width // block
    inner = 16
    dim = width // H
    row_count = front.shape[0]
    hist_width = width // 2
    owned = lengths.shape[0]
    shift = owned * own_events
    group_rows = 2 * shift
    sources = row_count // group_rows
    scale = 1.0 / math.sqrt(dim)

    def kernel(
        place_ref, len_ref, front_ref, front_other_ref, dense_hbm, cot_hbm, req_ref, *rest
    ):
        mine_refs, other_refs = rest[:2], rest[2:4]
        out_ref, back_ref, wq_ref, wo_ref, ev_ref, cot_ref, dense_ref, cot_sem, dense_sem = rest[4:]
        cot_copy = pltpu.make_async_copy(cot_hbm, cot_ref, cot_sem)
        dense_copy = pltpu.make_async_copy(dense_hbm, dense_ref, dense_sem)
        dense_copy.start()
        cot_copy.start()
        x = place_ref[1]

        def place(pieces, target):
            near, far = pieces
            for piece, offset in ((near.at[0], 0), (near.at[1], outer - 1), (near.at[2], 1), (far, 2)):
                for i in range(block // inner):
                    start = pl.multiple_of((i * outer + lax.rem(x + offset, outer)) * inner, inner)
                    target[pl.ds(start, inner), :] = piece[i * inner : (i + 1) * inner, :]

        @pl.when(place_ref[0] == 0)
        def _():
            place(mine_refs, wq_ref)
            place(other_refs, wo_ref)
            ev_ref[:, :hist_width] = front_ref[:, :hist_width]
            ev_ref[:, hist_width:] = front_other_ref[:, :hist_width]

        @pl.when(place_ref[0] != 0)
        def _():
            place(other_refs, wq_ref)
            place(mine_refs, wo_ref)
            ev_ref[:, :hist_width] = front_other_ref[:, :hist_width]
            ev_ref[:, hist_width:] = front_ref[:, :hist_width]

        parts = [
            front_ref[:, hist_width + p * cands : hist_width + (p + 1) * cands].astype(jnp.float32) for p in range(2)
        ]
        pooled = jnp.concatenate(
            [parts[p][t * group_rows : (t + 1) * group_rows, :] for t in range(sources) for p in range(2)], axis=0
        )
        pooled = jnp.transpose(pooled)
        dense_copy.wait()
        query_pre = dot_nn(pooled.astype(jnp.bfloat16), wq_ref[:pooled_width, :]) + dot_nn(
            dense_ref[...], wq_ref[pooled_width:, :]
        )
        gate = jax.nn.sigmoid(query_pre)
        query = (query_pre * gate).astype(jnp.bfloat16)
        query_slope = gate * (1.0 + query_pre * (1.0 - gate))

        index = lax.broadcasted_iota(jnp.int32, (cands, row_count), 1)
        within = index % group_rows
        owner = within // own_events
        time = index // group_rows * own_events + within % own_events
        limit = jnp.full((cands, row_count), len_ref[0], jnp.int32)
        for a in range(1, owned):
            limit = jnp.where(owner == a, len_ref[a], limit)
        request = jnp.transpose(jnp.broadcast_to(req_ref[...].astype(jnp.float32), (cands, cands))).astype(jnp.int32)
        request = jnp.concatenate([request] * (row_count // cands), axis=1)
        live = (owner == request) & (time < limit)

        weights, slopes, attended = [], [], []
        for h in range(H):
            cols = slice(h * dim, (h + 1) * dim)
            score = dot_nt(query[:, cols], ev_ref[:, cols]) * scale
            sig = jax.nn.sigmoid(score)
            weight = jnp.where(live, score * sig, 0.0)
            weights.append(pltpu.roll(weight, shift, 1).astype(jnp.bfloat16))
            slopes.append(jnp.where(live, sig * (1.0 + score * (1.0 - sig)) * scale, 0.0))
            attended.append(dot_nn(weights[h], ev_ref[:, cols]))
        attended = jnp.concatenate(attended, axis=1)
        centered = attended - jnp.mean(attended, axis=1, keepdims=True)
        inverse = lax.rsqrt(jnp.mean(centered * centered, axis=1, keepdims=True) + norm_eps)
        normed = centered * inverse
        mixed = dot_nn(normed.astype(jnp.bfloat16), wo_ref[...])
        out_ref[:, :pooled_width] = (mixed[:, :pooled_width] + pooled).astype(jnp.bfloat16)
        out_ref[:, pooled_width:] = (mixed[:, pooled_width:] + dense_ref[...].astype(jnp.float32)).astype(
            jnp.bfloat16
        )
        cot_copy.wait()
        back_y = dot_nt(cot_ref[...], wo_ref[...])
        back_att = inverse * (
            back_y
            - jnp.mean(back_y, axis=1, keepdims=True)
            - normed * jnp.mean(back_y * normed, axis=1, keepdims=True)
        )
        back_att = back_att.astype(jnp.bfloat16)
        back_query = []
        for h in range(H):
            cols = slice(h * dim, (h + 1) * dim)
            back_w = dot_nt(back_att[:, cols], ev_ref[:, cols])
            back_w = pltpu.roll(back_w, row_count - shift, 1)
            back_s = (back_w * slopes[h]).astype(jnp.bfloat16)
            back_query.append(dot_nn(back_s, ev_ref[:, cols]))
            back_ref[:, cols] = dot_tn(
                jnp.concatenate([back_s, weights[h]], axis=0),
                jnp.concatenate([query[:, cols], back_att[:, cols]], axis=0),
            ).astype(jnp.bfloat16)
        back_pre = (jnp.concatenate(back_query, axis=1) * query_slope).astype(jnp.bfloat16)
        pool = jnp.transpose(cot_ref[:, :pooled_width].astype(jnp.float32)) + dot_nt(
            wq_ref[:pooled_width, :], back_pre
        )
        for p in range(2):
            part = jnp.concatenate(
                [
                    pool[(2 * t + p) * group_rows : (2 * t + p + 1) * group_rows, :]
                    for t in range(sources)
                ],
                axis=0,
            )
            back_ref[:, width + p * cands : width + (p + 1) * cands] = part.astype(jnp.bfloat16)

    vmem = pl.BlockSpec(memory_space=pltpu.VMEM)
    smem = pl.BlockSpec(memory_space=pltpu.SMEM)
    hbm = pl.BlockSpec(memory_space=pltpu.HBM)
    return pl.pallas_call(
        kernel,
        in_specs=[smem, smem, vmem, vmem, hbm, hbm] + [vmem] * 5,
        out_specs=[vmem] * 2,
        out_shape=[
            jax.ShapeDtypeStruct((cands, width), jnp.bfloat16),
            jax.ShapeDtypeStruct((row_count, width + 2 * cands), jnp.bfloat16),
        ],
        scratch_shapes=[pltpu.VMEM((width, width), jnp.bfloat16)] * 2
        + [
            pltpu.VMEM((row_count, width), jnp.bfloat16),
            pltpu.VMEM((cands, width), jnp.bfloat16),
            pltpu.VMEM((cands, dense_width), jnp.bfloat16),
            pltpu.SemaphoreType.DMA,
            pltpu.SemaphoreType.DMA,
        ],
        compiler_params=pltpu.CompilerParams(vmem_limit_bytes=40 << 20),
        cost_estimate=pl.CostEstimate(
            flops=8 * cands * width * width, bytes_accessed=8 * width * width, transcendentals=0
        ),
        name="layer",
    )(
        place_index,
        lengths,
        front,
        front_other,
        pltpu.with_memory_space_constraint(dense, pltpu.HBM),
        pltpu.with_memory_space_constraint(cot, pltpu.HBM),
        requests,
        *mine,
        *other,
    )


def on_device(dense_feat, emb_ids, tables, history_kv, hist_len, cand_request, w_query, w_out, cotangent):
    _, emb_width, _ = tables.shape
    sizes = {a: lax.axis_size(a) for a in ALL}
    cand_devices = sizes["x"] * sizes["yl"] * sizes["core"]
    own_rows, model_width = w_query.shape
    owned, own_events, _ = history_kv.shape
    group = emb_ids.shape[2]
    cands = group // cand_devices
    ring = sizes["x"]
    up = [(i, (i + 1) % ring) for i in range(ring)]
    down = [(i, (i - 1) % ring) for i in range(ring)]
    swap = [(0, 1), (1, 0)]

    slab = sizes["yh"] * sizes["z"] * sizes["yl"]
    own = jnp.concatenate([w_query, w_out], axis=0).reshape(1, 2, own_rows, model_width)
    own = jnp.broadcast_to(own, (slab, 2, own_rows, model_width)).reshape(2 * slab, own_rows, model_width)
    w1 = lax.all_to_all(own, ("yh", "z", "yl", "core"), 0, 0)
    w1 = lax.optimization_barrier(w1.reshape(-1, model_width))

    history = jnp.transpose(history_kv.reshape(owned, own_events, 2, model_width), (2, 0, 1, 3))
    history = history.reshape(-1, model_width)
    early = group // 8 * 7
    blocks = lookup(emb_ids[0], tables[0], history, cands, 0, early)

    left = lax.ppermute(w1, "x", up)
    right = lax.ppermute(w1, "x", down)
    blocks = lookup(emb_ids[0], tables[0], history, cands, early, group - early, blocks)

    front = lax.all_to_all(blocks, CAND, 0, 0)
    front = front.reshape(-1, front.shape[2])
    front_other = lax.ppermute(front, "core", swap)

    both_ways = [(2 * i, 2 * ((i + 1) % ring)) for i in range(ring)] + [
        (2 * i + 1, 2 * ((i - 1) % ring) + 1) for i in range(ring)
    ]
    passed = jnp.where(lax.axis_index("core") == 0, left, right)
    far = lax.ppermute(passed, ("x", "core"), both_ways)
    near = jnp.stack([w1, left, right])
    near_other = lax.ppermute(near, "core", swap)
    far_other = lax.ppermute(far, "core", swap)

    cand_out, back = layer(
        front,
        front_other,
        dense_feat,
        cotangent,
        (near, far),
        (near_other, far_other),
        jnp.stack([lax.axis_index("core"), lax.axis_index("x")]),
        cand_request.reshape(1, -1),
        hist_len,
        own_events,
    )

    back = lax.all_to_all(back.reshape(cand_devices, -1, back.shape[1]), CAND, 0, 0)
    d_kv = jnp.sum(back[:, :, :model_width].astype(jnp.float32), axis=0)
    d_kv = jnp.transpose(d_kv.reshape(2, owned, own_events, model_width), (1, 2, 0, 3))
    d_kv = d_kv.reshape(owned, own_events, 2 * model_width)
    pool = back[:, :, model_width:].reshape(cand_devices, -1, 2, cands)
    d_pooled = jnp.transpose(pool, (2, 1, 0, 3)).reshape(1, emb_width, group)
    return cand_out, d_kv, d_pooled


def solution(mesh):
    parts = Mesh(mesh.devices.reshape(2, 8, 4, 4, 2), ALL)
    rows = P(ALL, None)
    return jax.shard_map(
        on_device,
        mesh=parts,
        in_specs=(
            rows,
            P(CAND, None, REQ),
            P(CAND, None, None),
            P(REQ, CAND, None),
            P(REQ),
            P(ALL),
            rows,
            rows,
            rows,
        ),
        out_specs=(rows, P(REQ, CAND, None), P(CAND, None, REQ)),
        check_vma=False,
    )
```

```python
import math

import jax
import jax.numpy as jnp
from jax import lax
from jax.experimental import pallas as pl
from jax.experimental.pallas import tpu as pltpu
from jax.sharding import Mesh, PartitionSpec as P


H = 8
norm_eps = 1e-05

REQ = ("yh", "z")
CAND = ("x", "yl", "core")
ALL = REQ + CAND


LOW = 512
TILE = 256


def lookup(ids, table, history, cands, first, count, into=None):
    bag, total_count = ids.shape
    emb, rows = table.shape
    hist_rows = history.shape[0]
    hist_width = history.shape[1] // 2
    highs = rows // LOW
    step = min(count, 2 * TILE)
    half = emb // 2

    def kernel(ids_hbm, table_ref, history_ref, *rest):
        out_ref, stacked_ref, ids_ref, ids_sem = rest[-4:]

        @pl.when(pl.program_id(0) == 0)
        def _():
            ids_copy = pltpu.make_async_copy(ids_hbm.at[:, pl.ds(first, count)], ids_ref, ids_sem)
            ids_copy.start()
            for high in range(highs):
                stacked_ref[high * emb : (high + 1) * emb, :] = table_ref[:, high * LOW : (high + 1) * LOW]
            ids_copy.wait()

        offset = pl.program_id(0) * step
        low_iota = lax.broadcasted_iota(jnp.int32, (LOW, TILE), 0)
        for run in range(step // cands):
            core = run % 2
            out_ref[run, :, :hist_width] = history_ref[:, core * hist_width : (core + 1) * hist_width]
        for tile in range(step // TILE):
            span = pl.ds(pl.multiple_of(offset + tile * TILE, TILE), TILE)
            total = jnp.zeros((emb, TILE), jnp.float32)
            for slot in range(bag):
                row = ids_ref[slot : slot + 1, span]
                low = jnp.bitwise_and(row, LOW - 1)
                high_of = jnp.broadcast_to(jnp.right_shift(row, LOW.bit_length() - 1), (emb, TILE))
                one_hot = (low_iota == low).astype(jnp.float32).astype(jnp.bfloat16)
                picked = jnp.dot(stacked_ref[...], one_hot, preferred_element_type=jnp.float32)
                found = jnp.zeros((emb, TILE), jnp.float32)
                for high in range(highs):
                    found = jnp.where(high_of == high, picked[high * emb : (high + 1) * emb, :], found)
                total = total + found
            for run in range(TILE // cands):
                cols = slice(run * cands, (run + 1) * cands)
                for part in range(2):
                    column = hist_width + part * cands
                    out_ref[tile * (TILE // cands) + run, :, column : column + cands] = total[
                        part * half : (part + 1) * half, cols
                    ].astype(jnp.bfloat16)

    width = hist_width + 2 * cands
    hbm = pl.BlockSpec(memory_space=pltpu.HBM)
    arguments = (pltpu.with_memory_space_constraint(ids, pltpu.HBM), table, history)
    return pl.pallas_call(
        kernel,
        grid=(count // step,),
        in_specs=[
            hbm,
            pl.BlockSpec((emb, rows), lambda i: (0, 0)),
            pl.BlockSpec(history.shape, lambda i: (0, 0)),
        ]
        + ([] if into is None else [hbm]),
        out_specs=pl.BlockSpec((step // cands, hist_rows, width), lambda i: (first // step + i, 0, 0)),
        out_shape=jax.ShapeDtypeStruct((total_count // cands, hist_rows, width), jnp.bfloat16),
        input_output_aliases={} if into is None else {3: 0},
        scratch_shapes=[
            pltpu.VMEM((highs * emb, LOW), jnp.bfloat16),
            pltpu.VMEM((bag, count), jnp.int32),
            pltpu.SemaphoreType.DMA,
        ],
        compiler_params=pltpu.CompilerParams(vmem_limit_bytes=32 << 20),
        cost_estimate=pl.CostEstimate(
            flops=2 * emb * rows * bag * count, bytes_accessed=2 * emb * rows, transcendentals=0
        ),
        name="lookup",
    )(*arguments, *(() if into is None else (into,)))


def dot_nn(left, right):
    return jnp.dot(left, right, preferred_element_type=jnp.float32)


def dot_nt(left, right):
    return lax.dot_general(left, right, (((1,), (1,)), ((), ())), preferred_element_type=jnp.float32)


def dot_tn(left, right):
    return lax.dot_general(left, right, (((0,), (0,)), ((), ())), preferred_element_type=jnp.float32)


def layer(front, front_other, dense, cot, mine, other, place_index, requests, lengths, own_events):
    cands, dense_width = dense.shape
    block, width = mine[1].shape
    pooled_width = width - dense_width
    outer = width // block
    inner = 16
    dim = width // H
    row_count = front.shape[0]
    hist_width = width // 2
    owned = lengths.shape[0]
    shift = owned * own_events
    group_rows = 2 * shift
    sources = row_count // group_rows
    scale = 1.0 / math.sqrt(dim)

    def kernel(
        place_ref, len_ref, front_ref, front_other_ref, dense_hbm, cot_hbm, req_ref, *rest
    ):
        mine_refs, other_refs = rest[:2], rest[2:4]
        out_ref, back_ref, wq_ref, wo_ref, ev_ref, cot_ref, dense_ref, cot_sem, dense_sem = rest[4:]
        cot_copy = pltpu.make_async_copy(cot_hbm, cot_ref, cot_sem)
        dense_copy = pltpu.make_async_copy(dense_hbm, dense_ref, dense_sem)
        dense_copy.start()
        cot_copy.start()
        x = place_ref[1]

        def place(pieces, target, first, second):
            near, far = pieces
            for piece, offset in ((near.at[0], 0), (near.at[1], first), (near.at[2], second), (far, 2)):
                for i in range(block // inner):
                    start = pl.multiple_of((i * outer + lax.rem(x + offset, outer)) * inner, inner)
                    target[pl.ds(start, inner), :] = piece[i * inner : (i + 1) * inner, :]

        @pl.when(place_ref[0] == 0)
        def _():
            place(mine_refs, wq_ref, outer - 1, 1)
            place(other_refs, wo_ref, 1, outer - 1)
            ev_ref[:, :hist_width] = front_ref[:, :hist_width]
            ev_ref[:, hist_width:] = front_other_ref[:, :hist_width]

        @pl.when(place_ref[0] != 0)
        def _():
            place(other_refs, wq_ref, outer - 1, 1)
            place(mine_refs, wo_ref, 1, outer - 1)
            ev_ref[:, :hist_width] = front_other_ref[:, :hist_width]
            ev_ref[:, hist_width:] = front_ref[:, :hist_width]

        parts = [
            front_ref[:, hist_width + p * cands : hist_width + (p + 1) * cands].astype(jnp.float32) for p in range(2)
        ]
        pooled = jnp.concatenate(
            [parts[p][t * group_rows : (t + 1) * group_rows, :] for t in range(sources) for p in range(2)], axis=0
        )
        pooled = jnp.transpose(pooled)
        dense_copy.wait()
        query_pre = dot_nn(pooled.astype(jnp.bfloat16), wq_ref[:pooled_width, :]) + dot_nn(
            dense_ref[...], wq_ref[pooled_width:, :]
        )
        gate = jax.nn.sigmoid(query_pre)
        query = (query_pre * gate).astype(jnp.bfloat16)
        query_slope = gate * (1.0 + query_pre * (1.0 - gate))

        index = lax.broadcasted_iota(jnp.int32, (cands, row_count), 1)
        within = index % group_rows
        owner = within // own_events
        time = index // group_rows * own_events + within % own_events
        limit = jnp.full((cands, row_count), len_ref[0], jnp.int32)
        for a in range(1, owned):
            limit = jnp.where(owner == a, len_ref[a], limit)
        request = jnp.transpose(jnp.broadcast_to(req_ref[...].astype(jnp.float32), (cands, cands))).astype(jnp.int32)
        request = jnp.concatenate([request] * (row_count // cands), axis=1)
        live = (owner == request) & (time < limit)

        weights, slopes, attended = [], [], []
        for h in range(H):
            cols = slice(h * dim, (h + 1) * dim)
            score = dot_nt(query[:, cols], ev_ref[:, cols]) * scale
            sig = jax.nn.sigmoid(score)
            weight = jnp.where(live, score * sig, 0.0)
            weights.append(pltpu.roll(weight, shift, 1).astype(jnp.bfloat16))
            slopes.append(jnp.where(live, sig * (1.0 + score * (1.0 - sig)) * scale, 0.0))
            attended.append(dot_nn(weights[h], ev_ref[:, cols]))
        attended = jnp.concatenate(attended, axis=1)
        centered = attended - jnp.mean(attended, axis=1, keepdims=True)
        inverse = lax.rsqrt(jnp.mean(centered * centered, axis=1, keepdims=True) + norm_eps)
        normed = centered * inverse
        mixed = dot_nn(normed.astype(jnp.bfloat16), wo_ref[...])
        out_ref[:, :pooled_width] = (mixed[:, :pooled_width] + pooled).astype(jnp.bfloat16)
        out_ref[:, pooled_width:] = (mixed[:, pooled_width:] + dense_ref[...].astype(jnp.float32)).astype(
            jnp.bfloat16
        )
        cot_copy.wait()
        back_y = dot_nt(cot_ref[...], wo_ref[...])
        back_att = inverse * (
            back_y
            - jnp.mean(back_y, axis=1, keepdims=True)
            - normed * jnp.mean(back_y * normed, axis=1, keepdims=True)
        )
        back_att = back_att.astype(jnp.bfloat16)
        back_query = []
        for h in range(H):
            cols = slice(h * dim, (h + 1) * dim)
            back_w = dot_nt(back_att[:, cols], ev_ref[:, cols])
            back_w = pltpu.roll(back_w, row_count - shift, 1)
            back_s = (back_w * slopes[h]).astype(jnp.bfloat16)
            back_query.append(dot_nn(back_s, ev_ref[:, cols]))
            back_ref[:, cols] = dot_tn(
                jnp.concatenate([back_s, weights[h]], axis=0),
                jnp.concatenate([query[:, cols], back_att[:, cols]], axis=0),
            ).astype(jnp.bfloat16)
        back_pre = (jnp.concatenate(back_query, axis=1) * query_slope).astype(jnp.bfloat16)
        pool = jnp.transpose(cot_ref[:, :pooled_width].astype(jnp.float32)) + dot_nt(
            wq_ref[:pooled_width, :], back_pre
        )
        for p in range(2):
            part = jnp.concatenate(
                [
                    pool[(2 * t + p) * group_rows : (2 * t + p + 1) * group_rows, :]
                    for t in range(sources)
                ],
                axis=0,
            )
            back_ref[:, width + p * cands : width + (p + 1) * cands] = part.astype(jnp.bfloat16)

    vmem = pl.BlockSpec(memory_space=pltpu.VMEM)
    smem = pl.BlockSpec(memory_space=pltpu.SMEM)
    hbm = pl.BlockSpec(memory_space=pltpu.HBM)
    return pl.pallas_call(
        kernel,
        in_specs=[smem, smem, vmem, vmem, hbm, hbm] + [vmem] * 5,
        out_specs=[vmem] * 2,
        out_shape=[
            jax.ShapeDtypeStruct((cands, width), jnp.bfloat16),
            jax.ShapeDtypeStruct((row_count, width + 2 * cands), jnp.bfloat16),
        ],
        scratch_shapes=[pltpu.VMEM((width, width), jnp.bfloat16)] * 2
        + [
            pltpu.VMEM((row_count, width), jnp.bfloat16),
            pltpu.VMEM((cands, width), jnp.bfloat16),
            pltpu.VMEM((cands, dense_width), jnp.bfloat16),
            pltpu.SemaphoreType.DMA,
            pltpu.SemaphoreType.DMA,
        ],
        compiler_params=pltpu.CompilerParams(vmem_limit_bytes=40 << 20),
        cost_estimate=pl.CostEstimate(
            flops=8 * cands * width * width, bytes_accessed=8 * width * width, transcendentals=0
        ),
        name="layer",
    )(
        place_index,
        lengths,
        front,
        front_other,
        pltpu.with_memory_space_constraint(dense, pltpu.HBM),
        pltpu.with_memory_space_constraint(cot, pltpu.HBM),
        requests,
        *mine,
        *other,
    )


def on_device(dense_feat, emb_ids, tables, history_kv, hist_len, cand_request, w_query, w_out, cotangent):
    _, emb_width, _ = tables.shape
    sizes = {a: lax.axis_size(a) for a in ALL}
    cand_devices = sizes["x"] * sizes["yl"] * sizes["core"]
    own_rows, model_width = w_query.shape
    owned, own_events, _ = history_kv.shape
    group = emb_ids.shape[2]
    cands = group // cand_devices
    ring = sizes["x"]
    swap = [(0, 1), (1, 0)]

    slab = sizes["yh"] * sizes["z"] * sizes["yl"]
    own = jnp.concatenate([w_query, w_out], axis=0).reshape(1, 2, own_rows, model_width)
    own = jnp.broadcast_to(own, (slab, 2, own_rows, model_width)).reshape(2 * slab, own_rows, model_width)
    w1 = lax.all_to_all(own, ("yh", "z", "yl", "core"), 0, 0)
    w1 = lax.optimization_barrier(w1.reshape(-1, model_width))

    history = jnp.transpose(history_kv.reshape(owned, own_events, 2, model_width), (2, 0, 1, 3))
    history = history.reshape(-1, model_width)
    early = group // 8 * 7
    blocks = lookup(emb_ids[0], tables[0], history, cands, 0, early)

    outward = [(2 * i, 2 * ((i + 1) % ring)) for i in range(ring)] + [
        (2 * i + 1, 2 * ((i - 1) % ring) + 1) for i in range(ring)
    ]
    inward = [(target, source) for source, target in outward]
    side_a = lax.ppermute(w1, ("x", "core"), outward)
    side_b = lax.ppermute(w1, ("x", "core"), inward)

    blocks = lookup(emb_ids[0], tables[0], history, cands, early, group - early, blocks)

    front = lax.all_to_all(blocks, CAND, 0, 0)
    front = front.reshape(-1, front.shape[2])
    front_other = lax.ppermute(front, "core", swap)

    far = lax.ppermute(side_a, ("x", "core"), outward)
    near = jnp.stack([w1, side_a, side_b])
    near_other = lax.ppermute(near, "core", swap)
    far_other = lax.ppermute(far, "core", swap)

    cand_out, back = layer(
        front,
        front_other,
        dense_feat,
        cotangent,
        (near, far),
        (near_other, far_other),
        jnp.stack([lax.axis_index("core"), lax.axis_index("x")]),
        cand_request.reshape(1, -1),
        hist_len,
        own_events,
    )

    back = lax.all_to_all(back.reshape(cand_devices, -1, back.shape[1]), CAND, 0, 0)
    d_kv = jnp.sum(back[:, :, :model_width].astype(jnp.float32), axis=0)
    d_kv = jnp.transpose(d_kv.reshape(2, owned, own_events, model_width), (1, 2, 0, 3))
    d_kv = d_kv.reshape(owned, own_events, 2 * model_width)
    pool = back[:, :, model_width:].reshape(cand_devices, -1, 2, cands)
    d_pooled = jnp.transpose(pool, (2, 1, 0, 3)).reshape(1, emb_width, group)
    return cand_out, d_kv, d_pooled


def solution(mesh):
    parts = Mesh(mesh.devices.reshape(2, 8, 4, 4, 2), ALL)
    rows = P(ALL, None)
    return jax.shard_map(
        on_device,
        mesh=parts,
        in_specs=(
            rows,
            P(CAND, None, REQ),
            P(CAND, None, None),
            P(REQ, CAND, None),
            P(REQ),
            P(ALL),
            rows,
            rows,
            rows,
        ),
        out_specs=(rows, P(REQ, CAND, None), P(CAND, None, REQ)),
        check_vma=False,
    )
```
